32 devices in a mesh: grp: 4 (over y, x), gx: 4 (over z), gy: 2 (over core).
Axes of the slice: x: 2, y: 2, z: 4, core: 2. Of those that a mesh axis runs over, the one named last changes fastest.
Arguments:
- coarse_modes: float32 [4, 2, 8, 32, 4096], P('grp', None, None, 'gy', 'gx'), may hold values from -6 to 6
- salinity: float32 [32, 128, 16384], P('grp', 'gy', 'gx'), may hold values from -6 to 6
- viscosity: float32 [4], P('grp'), may hold values from 0.1 to 1
- forcing_gain: float32 [4], P('grp'), may hold values from 0.5 to 2
- diffusivity: float32 [32], P('grp'), may hold values from 0.3 to 1.5
Outputs:
- salinity_next: float32 [32, 128, 16384], P('grp', 'gy', 'gx')
- coarse_next: float32 [4, 2, 8, 32, 4096], P('grp', None, None, 'gy', 'gx')
The draws below stay inside these ranges and needn't reach their ends.
All inputs are finite; a program needn't handle non-finite values.
Results may differ from the reference program's by a relative error of at most 0.0003.
Values sent between devices are 32-bit elements; how exact they have to be, the bound alone decides.
A program may use at most 192 MiB of HBM per device.

```python
import math
import jax
import jax.numpy as jnp
from jax import lax

FIELDS = 4
NV = 4096
RATIO = 4
LV = 8
NYC = 32
NZF = 32
NYF = 128
NXF = 16384


def shard_levels(own_key, dims, split, low, high):
    def one(dim, parts):
        draws = jax.random.uniform(jax.random.fold_in(jax.random.fold_in(own_key, 6), dim), (parts,), jnp.float32, low / len(split), high / len(split))
        return jnp.repeat(jnp.exp(draws), dims[dim] // parts).reshape((-1,) + (1,) * (len(dims) - dim - 1))

    gain = one(*split[0])
    for cut in split[1:]:
        gain = gain * one(*cut)
    return gain


def noise(stream_key, shape, scale, reach, shards=(), kind=jnp.bfloat16):
    entries = jax.random.normal(stream_key, shape, jnp.float32) * scale
    if len(shards) > 0:
        entries = shard_levels(stream_key, shape, shards, -0.22, 0.18) * entries
    return jnp.clip(entries, min=-reach, max=reach).astype(kind)


def setup_inputs(seed: int = 0) -> dict:
    splits = jax.random.split(jax.random.key(seed), 6)
    return {
        "coarse_modes": noise(splits[0], (FIELDS, 2, LV, NYC, NV), 1.0, 6.0, ((0, 4), (3, 2), (4, 4)), jnp.float32),
        "salinity": noise(splits[1], (NZF, NYF, NXF), 1.0, 6.0, ((0, 4), (1, 2), (2, 4)), jnp.float32),
        "viscosity": jnp.clip(jnp.exp(math.log(1.0) - 2.3025851 * jax.random.uniform(splits[2], (FIELDS,), jnp.float32) ** shard_levels(splits[2], (FIELDS,), ((0, 4),), -0.2, 0.2)), 0.1, 1.0),
        "forcing_gain": jnp.clip(0.5 + 1.5 * jax.random.uniform(splits[3], (FIELDS,), jnp.float32) ** shard_levels(splits[3], (FIELDS,), ((0, 4),), -0.2, 0.2), 0.5, 2.0),
        "diffusivity": jnp.clip(jnp.exp(math.log(1.5) - 1.60943787 * jax.random.uniform(splits[4], (NZF,), jnp.float32) ** shard_levels(splits[4], (NZF,), ((0, 4),), -0.2, 0.2)), 0.3, 1.5),
    }


fine_step = 0.1


def refine(coarse, dimension):
    extent = coarse.shape[dimension]
    pieces = []
    for sub_cell in range(RATIO):
        offset = (sub_cell + 0.5) / RATIO - 0.5
        beside = jnp.roll(coarse, -1 if offset > 0 else 1, axis=dimension)
        pieces.append((1.0 - abs(offset)) * coarse + abs(offset) * beside)
    stacked = jnp.stack(pieces, axis=dimension + 1)
    target = list(coarse.shape)
    target[dimension] = extent * RATIO
    return stacked.reshape(target)


def reference(coarse_modes, salinity, viscosity, forcing_gain, diffusivity):
    spectral = lax.complex(coarse_modes[:, 0], coarse_modes[:, 1])
    physical = jnp.real(jnp.fft.ifft(spectral, axis=-1, norm="ortho"))

    def update(fine_level):
        coarse_plane = lax.dynamic_index_in_dim(physical, fine_level // RATIO, 1, keepdims=False)
        velocity = refine(refine(coarse_plane, 1), 2)
        centre = lax.dynamic_index_in_dim(salinity, fine_level, 0, keepdims=False)
        upper_cells = lax.dynamic_index_in_dim(salinity, (fine_level + 1) % NZF, 0, keepdims=False)
        lower_cells = lax.dynamic_index_in_dim(salinity, (fine_level + NZF - 1) % NZF, 0, keepdims=False)
        east_cells = jnp.roll(centre, -1, axis=1)
        west_cells = jnp.roll(centre, 1, axis=1)
        north_cells = jnp.roll(centre, -1, axis=0)
        south_cells = jnp.roll(centre, 1, axis=0)
        diffuse_rate = lax.dynamic_index_in_dim(diffusivity, fine_level, 0, keepdims=False)
        spread = diffuse_rate * (east_cells + west_cells + north_cells + south_cells + upper_cells + lower_cells - 6.0 * centre)
        advection = velocity[0] * (east_cells - west_cells) * 0.5 + velocity[1] * (north_cells - south_cells) * 0.5 + velocity[2] * (upper_cells - lower_cells) * 0.5
        updated = centre + fine_step * (spread - advection)
        buoyancy = velocity[3] - updated
        restricted = buoyancy.reshape(NYC, RATIO, NV, RATIO).mean(axis=(1, 3))
        return updated, restricted

    salinity_next, restricted = lax.map(update, jnp.arange(NZF, dtype=jnp.int32))
    buoyancy = restricted.reshape(LV, RATIO, NYC, NV).mean(axis=1)
    spectrum = jnp.fft.fft(buoyancy, axis=-1, norm="ortho")
    spectral_parts = jnp.stack([jnp.real(spectrum), jnp.imag(spectrum)])
    mode_index = jnp.arange(NV, dtype=jnp.int32)
    wavenumber = jnp.where(mode_index < NV // 2, mode_index, mode_index - NV)
    scaled_wave = (2.0 * math.pi / NV) * wavenumber.astype(jnp.float32)
    damping = jnp.exp(-viscosity[:, None] * scaled_wave[None, :] * scaled_wave[None, :])
    coarse_next = damping[:, None, None, None, :] * coarse_modes + forcing_gain[:, None, None, None, None] * spectral_parts[None]
    return salinity_next, coarse_next
```

```python
import math

import jax
import jax.numpy as jnp
import numpy as np
from jax import lax
from jax.experimental import pallas as pl
from jax.experimental.pallas import tpu as pltpu
from jax.sharding import PartitionSpec as P

RATIO = 4


fine_step = 0.1


LANES = 128
SUBLANES = 8
MESH = pl.DeviceIdType.MESH


def turn_table(rows, cols, period, orient, shift):
    product = np.outer(np.arange(rows) - shift, np.arange(cols)) % period
    angle = 2.0 * np.pi / period * product
    return np.cos(angle), orient * np.sin(angle)


def twist_table(length, orient, shift):
    cosine, sine = turn_table(length // LANES, LANES, length, orient, shift)
    return (np.stack([cosine, sine]) * length ** (-0.25)).astype(np.float32)


def lane_table(length, orient, want_imag):
    tiles = length // LANES
    groups = LANES // tiles
    order = (np.arange(tiles)[None, :] * groups + np.arange(groups)[:, None]).reshape(-1)
    cosine, sine = turn_table(LANES, LANES, LANES, orient, 0)
    cosine, sine = cosine[order], sine[order]
    table = np.concatenate([cosine, -sine], axis=1)
    if want_imag:
        table = np.concatenate([table, np.concatenate([sine, cosine], axis=1)], axis=0)
    table = (table * length ** (-0.25)).astype(np.float32)
    high = table.astype(jnp.bfloat16)
    low = (table - high.astype(np.float32)).astype(jnp.bfloat16)
    return np.concatenate([high, low, high], axis=1)


def butterflies(parts, orient):
    count = len(parts)
    if count == 1:
        return parts
    even = butterflies(parts[0::2], orient)
    odd = butterflies(parts[1::2], orient)
    sums, differences = [], []
    for k in range(count // 2):
        real, imag = odd[k]
        if k == 0:
            turned = (real, imag)
        elif 4 * k == count:
            turned = (None if imag is None else -orient * imag, orient * real)
        else:
            angle = orient * 2.0 * math.pi * k / count
            cosine, sine = math.cos(angle), math.sin(angle)
            if imag is None:
                turned = (cosine * real, sine * real)
            else:
                turned = (cosine * real - sine * imag, sine * real + cosine * imag)
        first = even[k]
        sums.append((plus(first[0], turned[0]), plus(first[1], turned[1])))
        differences.append((minus(first[0], turned[0]), minus(first[1], turned[1])))
    return sums + differences


def plus(left, right):
    if left is None:
        return right
    return left if right is None else left + right


def minus(left, right):
    if right is None:
        return left
    return -right if left is None else left - right


def split_stack(value):
    high, low = split_parts(value)
    return jnp.concatenate([high, high, low], axis=1)


def transform_lines(tiles, orient, shift, twist_ref, table_ref, mid_ref):
    count = len(tiles)
    bins = butterflies(tiles, orient)
    for r in range(count):
        real, imag = bins[(r - shift) % count]
        cosine, sine = twist_ref[0, r : r + 1, :], twist_ref[1, r : r + 1, :]
        at = slice(r * SUBLANES, (r + 1) * SUBLANES)
        if imag is None:
            mid_ref[0, at, :], mid_ref[1, at, :] = real * cosine, real * sine
        else:
            mid_ref[0, at, :] = real * cosine - imag * sine
            mid_ref[1, at, :] = real * sine + imag * cosine
    parts = [
        jnp.concatenate(
            [mid_ref[k, pl.ds(row, count, stride=SUBLANES), :] for row in range(SUBLANES)], axis=0
        )
        for k in range(2)
    ]
    stacked = split_stack(jnp.concatenate(parts, axis=1))
    return lax.dot_general(
        table_ref[...], stacked, (((1,), (1,)), ((), ())), preferred_element_type=jnp.float32
    )


def natural_tiles(result, count, turn_ref):
    groups = LANES // count
    group_at = lax.broadcasted_iota(jnp.int32, (count, LANES), 1) // count
    for tile in range(SUBLANES // groups):
        lanes = slice(tile * LANES, (tile + 1) * LANES)
        pieces = [result[k * count : (k + 1) * count, lanes] for k in range(groups)]
        for row in range(groups):
            line = None
            for k in range(groups):
                shift = count * (k - row) % LANES
                moved = pieces[k] if shift == 0 else pltpu.roll(pieces[k], shift, 1)
                line = moved if line is None else jnp.where(group_at == k, moved, line)
            start = (tile * groups + row) * count
            turn_ref[start : start + count, :] = line
    return [turn_ref[pl.ds(u, SUBLANES, stride=count), :] for u in range(count)]


def greet(groups, columns, neighbours):
    barrier = pltpu.get_barrier_semaphore()
    mine, at = lax.axis_index("grp"), lax.axis_index("gx")
    total = 0
    for d in range(groups):
        for e in range(columns):
            if d == 0 and e == 0:
                continue
            pl.semaphore_signal(
                barrier,
                inc=1,
                device_id={"grp": lax.rem(mine + d, groups), "gx": lax.rem(at + e, columns)},
                device_id_type=MESH,
            )
            total += 1
    for neighbour in neighbours:
        pl.semaphore_signal(barrier, inc=1, device_id={"gy": neighbour}, device_id_type=MESH)
        total += 1
    pl.semaphore_wait(barrier, total)


def forward_kernel(
    groups,
    columns,
    halves_y,
    modes_ref,
    twist_ref,
    table_ref,
    rim_ref,
    pencil,
    mid,
    turn,
    lines,
    landed,
    side_out,
    side_in,
    send_one,
    recv_one,
    own_sem,
    send_two,
    recv_two,
    side_send,
    side_recv,
):
    mine, at, half = lax.axis_index("grp"), lax.axis_index("gx"), lax.axis_index("gy")
    above, below = lax.rem(half + 1, halves_y), lax.rem(half + halves_y - 1, halves_y)
    planes, rows, width = modes_ref.shape[1:]
    quarter = planes // groups
    row_blocks = rows // SUBLANES
    blocks = quarter * row_blocks
    turns = pencil.shape[0]
    count = pencil.shape[3] // LANES
    span = width + LANES
    greet(groups, columns, (above, below))

    def place(block):
        group, inner = block // blocks, lax.rem(block, blocks)
        plane = inner // row_blocks
        row = pl.multiple_of(lax.rem(inner, row_blocks) * SUBLANES, SUBLANES)
        return group, inner, plane, row

    def first_copy(i, d):
        other = lax.rem(at + d, columns)
        group, _, plane, row = place(other + columns * i)
        source = modes_ref.at[:, group * quarter + plane, pl.ds(row, SUBLANES), :]
        target = pencil.at[i, :, :, pl.ds(pl.multiple_of(at * width, LANES), width)]
        if d == 0:
            return pltpu.make_async_copy(source, target, own_sem.at[i])
        return pltpu.make_async_remote_copy(
            src_ref=source,
            dst_ref=target,
            send_sem=send_one.at[i, d],
            recv_sem=recv_one.at[i, d],
            device_id={"gx": other},
            device_id_type=MESH,
        )

    for i in range(turns):
        for d in range(columns):
            first_copy(i, (d + 1) % columns).start()

    def second_copy(i, b):
        group, inner, plane, row = place(at + columns * i)
        source = lines.at[i, :, pl.ds(b * width, span)]
        target = landed.at[mine, plane, pl.ds(row, SUBLANES), :]
        remote = lambda: pltpu.make_async_remote_copy(
            src_ref=source,
            dst_ref=target,
            send_sem=send_two.at[i, b],
            recv_sem=recv_two.at[mine, inner],
            device_id={"grp": group, "gx": b},
            device_id_type=MESH,
        )
        local = lambda: pltpu.make_async_copy(source, target, recv_two.at[mine, inner])
        stays = jnp.logical_and(group == mine, at == b)
        return remote, local, stays

    def one_turn(i, carry):
        for d in range(columns):
            if d == 0:
                first_copy(i, 0).wait()
            else:
                first_copy(i, d).wait_recv()
        tiles = [
            tuple(pencil[i, k, :, p * LANES : (p + 1) * LANES] for k in range(2))
            for p in range(count)
        ]
        result = transform_lines(tiles, 1.0, 1, twist_ref, table_ref, mid)
        for u, tile in enumerate(natural_tiles(result, count, turn)):
            lines[i, :, u * LANES : (u + 1) * LANES] = tile
            if u == 0:
                lines[i, :, count * LANES : (count + 1) * LANES] = tile
        for b in range(columns):
            remote, local, stays = second_copy(i, b)
            pl.when(stays)(lambda: local().start())
            pl.when(jnp.logical_not(stays))(lambda: remote().start())
        return carry

    lax.fori_loop(0, turns, one_turn, 0)
    for field in range(groups):
        for inner in range(blocks):
            plane, row = inner // row_blocks, inner % row_blocks * SUBLANES
            target = landed.at[field, plane, pl.ds(row, SUBLANES), :]
            pltpu.make_async_copy(target, target, recv_two.at[field, inner]).wait()
    for field in range(groups):
        for plane in range(quarter):
            k = field * quarter + plane
            side_out[0, k : k + 1, :] = landed[field, plane, rows - 1 : rows, :]
            side_out[1, k : k + 1, :] = landed[field, plane, 0:1, :]
    sides = [
        pltpu.make_async_remote_copy(
            src_ref=side_out.at[k],
            dst_ref=side_in.at[k],
            send_sem=side_send.at[k],
            recv_sem=side_recv.at[k],
            device_id={"gy": (above, below)[k]},
            device_id_type=MESH,
        )
        for k in range(2)
    ]
    for side in sides:
        side.start()
    for field in range(groups):
        for plane in range(quarter):
            rim_ref[field, plane, 0:rows, :] = landed[field, plane]
    for side in sides:
        side.wait()
    rest = rim_ref.shape[2] - rows - 2
    for field in range(groups):
        for plane in range(quarter):
            k = field * quarter + plane
            tail = jnp.concatenate(
                [side_in[0, k : k + 1, :], side_in[1, k : k + 1, :], jnp.zeros((rest, span), jnp.float32)],
                axis=0,
            )
            rim_ref[field, plane, rows:, :] = tail
    for i in range(turns):
        for d in range(1, columns):
            first_copy(i, d).wait_send()
        for b in range(columns):
            remote, _, stays = second_copy(i, b)
            pl.when(jnp.logical_not(stays))(lambda: remote().wait_send())


def forward(modes, groups, columns, halves_y):
    _, planes, rows, width = modes.shape
    length = width * columns
    quarter = planes // groups
    blocks = quarter * (rows // SUBLANES)
    turns = groups * blocks // columns
    count = length // LANES
    span = width + LANES
    deep = -(-(rows + 2) // 16) * 16
    twist = twist_table(length, 1.0, 1)
    table = lane_table(length, 1.0, False)
    vmem = pl.BlockSpec(memory_space=pltpu.VMEM)
    dma = pltpu.SemaphoreType.DMA
    return pl.pallas_call(
        lambda *refs: forward_kernel(groups, columns, halves_y, *refs),
        name="forward_lines",
        out_shape=jax.ShapeDtypeStruct((groups, quarter, deep, span), jnp.float32),
        in_specs=[vmem] * 3,
        out_specs=vmem,
        scratch_shapes=[
            pltpu.VMEM((turns, 2, SUBLANES, length), jnp.float32),
            pltpu.VMEM((2, SUBLANES * count, LANES), jnp.float32),
            pltpu.VMEM((SUBLANES * count, LANES), jnp.float32),
            pltpu.VMEM((turns, SUBLANES, length + LANES), jnp.float32),
            pltpu.VMEM((groups, quarter, rows, span), jnp.float32),
            pltpu.VMEM((2, groups * quarter, span), jnp.float32),
            pltpu.VMEM((2, groups * quarter, span), jnp.float32),
            dma((turns, columns)),
            dma((turns, columns)),
            dma((turns,)),
            dma((turns, columns)),
            dma((groups, blocks)),
            dma((2,)),
            dma((2,)),
        ],
        compiler_params=pltpu.CompilerParams(
            collective_id=0, has_side_effects=True, vmem_limit_bytes=32 * 2**20
        ),
        cost_estimate=pl.CostEstimate(flops=10**9, bytes_accessed=10**8, transcendentals=0),
    )(modes, twist, table)


def backward_kernel(
    groups,
    columns,
    rates_ref,
    cells_ref,
    modes_ref,
    damp_ref,
    twist_ref,
    table_ref,
    out_ref,
    pencil,
    mid,
    turn,
    lines,
    spectrum,
    send_one,
    recv_one,
    send_two,
    recv_two,
    send_three,
):
    mine, at = lax.axis_index("grp"), lax.axis_index("gx")
    planes, rows, width = modes_ref.shape[1:]
    quarter = planes // groups
    row_blocks = rows // SUBLANES
    blocks = quarter * row_blocks
    slots = pencil.shape[0]
    count = pencil.shape[2] // LANES
    greet(groups, columns, ())

    def where_is(block):
        return block // row_blocks, block % row_blocks * SUBLANES

    def to_worker(block):
        worker, slot = block % columns, block // columns
        plane, row = where_is(block)
        source = cells_ref.at[plane, pl.ds(row, SUBLANES), :]
        target = pencil.at[slot, :, pl.ds(pl.multiple_of(at * width, LANES), width)]
        remote = lambda: pltpu.make_async_remote_copy(
            src_ref=source,
            dst_ref=target,
            send_sem=send_one.at[block],
            recv_sem=recv_one.at[slot, at],
            device_id={"gx": worker},
            device_id_type=MESH,
        )
        local = lambda: pltpu.make_async_copy(source, target, recv_one.at[slot, at])
        return remote, local, at == worker

    for block in range(blocks):
        remote, local, stays = to_worker(block)
        pl.when(stays)(lambda: local().start())
        pl.when(jnp.logical_not(stays))(lambda: remote().start())

    def to_owner(slot, b):
        block = at + columns * slot
        plane, row = block // row_blocks, lax.rem(block, row_blocks) * SUBLANES
        row = pl.multiple_of(row, SUBLANES)
        source = lines.at[slot, :, :, pl.ds(b * width, width)]
        target = spectrum.at[:, mine * quarter + plane, pl.ds(row, SUBLANES), :]
        remote = lambda: pltpu.make_async_remote_copy(
            src_ref=source,
            dst_ref=target,
            send_sem=send_two.at[slot, b],
            recv_sem=recv_two.at[mine, block],
            device_id={"gx": b},
            device_id_type=MESH,
        )
        local = lambda: pltpu.make_async_copy(source, target, recv_two.at[mine, block])
        return remote, local, at == b

    for slot in range(slots):

        def work(slot=slot):
            for e in range(columns):
                target = pencil.at[slot, :, pl.ds(e * width, width)]
                pltpu.make_async_copy(target, target, recv_one.at[slot, e]).wait()
            tiles = [(pencil[slot, :, u * LANES : (u + 1) * LANES], None) for u in range(count)]
            result = transform_lines(tiles, -1.0, 0, twist_ref, table_ref, mid)
            for k in range(2):
                part = result[k * LANES : (k + 1) * LANES]
                for u, tile in enumerate(natural_tiles(part, count, turn)):
                    lines[slot, k, :, u * LANES : (u + 1) * LANES] = tile
            for b in range(columns):
                remote, local, stays = to_owner(slot, b)
                pl.when(stays)(lambda: local().start())
                pl.when(jnp.logical_not(stays))(lambda: remote().start())

        if blocks % columns == 0:
            work()
        else:
            pl.when(at + columns * slot < blocks)(work)

    def arrival(group, block):
        plane, row = where_is(block)
        target = spectrum.at[:, group * quarter + plane, pl.ds(row, SUBLANES), :]
        return pltpu.make_async_copy(target, target, recv_two.at[group, block])

    def onward(block, d):
        plane, row = where_is(block)
        target = spectrum.at[:, mine * quarter + plane, pl.ds(row, SUBLANES), :]
        return pltpu.make_async_remote_copy(
            src_ref=target,
            dst_ref=target,
            send_sem=send_three.at[block, d],
            recv_sem=recv_two.at[mine, block],
            device_id={"grp": lax.rem(mine + d, groups)},
            device_id_type=MESH,
        )

    def finish(group, block):
        plane, row = where_is(block)
        index = group * quarter + plane
        for k in range(2):
            at_rows = pl.ds(row, SUBLANES)
            out_ref[k, index, at_rows, :] = (
                damp_ref[...] * modes_ref[k, index, at_rows, :]
                + rates_ref[0] * spectrum[k, index, at_rows, :]
            )

    for block in range(blocks):
        arrival(mine, block).wait()
        for d in range(1, groups):
            onward(block, d).start()
    for block in range(blocks):
        finish(mine, block)
    for block in range(blocks):
        for d in range(1, groups):
            group = lax.rem(mine + d, groups)
            arrival(group, block).wait()
            finish(group, block)
    for block in range(blocks):
        remote, _, stays = to_worker(block)
        pl.when(jnp.logical_not(stays))(lambda: remote().wait_send())
        for d in range(1, groups):
            onward(block, d).wait_send()
    for slot in range(slots):
        for b in range(columns):
            remote, _, stays = to_owner(slot, b)
            sent = jnp.logical_not(stays)
            if blocks % columns:
                sent = jnp.logical_and(sent, at + columns * slot < blocks)
            pl.when(sent)(lambda: remote().wait_send())


def backward(gain, cells, modes, damping, groups, columns):
    _, planes, rows, width = modes.shape
    length = width * columns
    quarter = planes // groups
    blocks = quarter * (rows // SUBLANES)
    slots = -(-blocks // columns)
    count = length // LANES
    twist = twist_table(length, -1.0, 0)
    table = lane_table(length, -1.0, True)
    vmem = pl.BlockSpec(memory_space=pltpu.VMEM)
    dma = pltpu.SemaphoreType.DMA
    return pl.pallas_call(
        lambda *refs: backward_kernel(groups, columns, *refs),
        name="backward_lines",
        out_shape=jax.ShapeDtypeStruct(modes.shape, jnp.float32),
        in_specs=[pl.BlockSpec(memory_space=pltpu.SMEM)] + [vmem] * 5,
        out_specs=vmem,
        scratch_shapes=[
            pltpu.VMEM((slots, SUBLANES, length), jnp.float32),
            pltpu.VMEM((2, SUBLANES * count, LANES), jnp.float32),
            pltpu.VMEM((SUBLANES * count, LANES), jnp.float32),
            pltpu.VMEM((slots, 2, SUBLANES, length), jnp.float32),
            pltpu.VMEM(modes.shape, jnp.float32),
            dma((blocks,)),
            dma((slots, columns)),
            dma((slots, columns)),
            dma((groups, blocks)),
            dma((blocks, groups)),
        ],
        compiler_params=pltpu.CompilerParams(
            collective_id=1, has_side_effects=True, vmem_limit_bytes=32 * 2**20
        ),
        cost_estimate=pl.CostEstimate(flops=10**9, bytes_accessed=5 * 10**7, transcendentals=0),
    )(gain, cells, modes, damping, twist, table)


def spread_table(cell_count, source_count):
    fine_count = cell_count * RATIO
    source = lax.broadcasted_iota(jnp.int32, (source_count, fine_count), 0)
    fine_cell = lax.broadcasted_iota(jnp.int32, (source_count, fine_count), 1)
    parent = fine_cell // RATIO
    sub_cell = (fine_cell % RATIO).astype(jnp.float32)
    offset = (sub_cell + 0.5) / RATIO - 0.5
    magnitude = jnp.abs(offset)
    own_weight = jnp.where(source == parent + 1, 1.0 - magnitude, 0.0)
    after_weight = jnp.where((source == parent + 2) & (offset > 0), magnitude, 0.0)
    before_weight = jnp.where((source == parent) & (offset < 0), magnitude, 0.0)
    return (own_weight + after_weight + before_weight).astype(jnp.bfloat16)


def rows_table(row_count, source_count):
    source = lax.broadcasted_iota(jnp.int32, (row_count * RATIO, source_count), 1)
    fine_row = lax.broadcasted_iota(jnp.int32, (row_count * RATIO, source_count), 0)
    parent = fine_row // RATIO
    offset = ((fine_row % RATIO).astype(jnp.float32) + 0.5) / RATIO - 0.5
    magnitude = jnp.abs(offset)
    before = jnp.where(parent == 0, row_count, parent - 1)
    after = jnp.where(parent == row_count - 1, row_count + 1, parent + 1)
    own_weight = jnp.where(source == parent, 1.0 - magnitude, 0.0)
    after_weight = jnp.where((source == after) & (offset > 0), magnitude, 0.0)
    before_weight = jnp.where((source == before) & (offset < 0), magnitude, 0.0)
    return (own_weight + after_weight + before_weight).astype(jnp.bfloat16)


def average_table(fine_count, weight):
    fine_cell = lax.broadcasted_iota(jnp.int32, (fine_count, fine_count // RATIO), 0)
    coarse_cell = lax.broadcasted_iota(jnp.int32, (fine_count, fine_count // RATIO), 1)
    return jnp.where(fine_cell // RATIO == coarse_cell, weight, 0.0).astype(jnp.bfloat16)


def split_parts(value):
    high = value.astype(jnp.bfloat16)
    return high, (value - high.astype(jnp.float32)).astype(jnp.bfloat16)


def product(left, right):
    return jnp.dot(left, right, preferred_element_type=jnp.float32)


def step_kernel(
    cells_coarse,
    diff_ref,
    centre_ref,
    below_ref,
    above_ref,
    lower_ref,
    upper_ref,
    south_ref,
    north_ref,
    west_ref,
    east_ref,
    rim_ref,
    ty_ref,
    tx_ref,
    ry_ref,
    rx_ref,
    out_ref,
    coarse_ref,
    vel_ref,
    acc_ref,
):
    level = pl.program_id(0)
    last = pl.num_programs(0) - 1
    part = lax.rem(level, RATIO)
    rows, cols = centre_ref.shape[1], centre_ref.shape[2]
    fine = cells_coarse * RATIO
    chunks = cols // fine
    span = tx_ref.shape[0]

    @pl.when(part == 0)
    def _():
        for field in range(rim_ref.shape[0]):
            high, low = split_parts(rim_ref[field, 0])
            along = product(ty_ref[...], high) + product(ty_ref[...], low)
            high, low = split_parts(along)
            for k in range(chunks):
                window = slice(k * cells_coarse, k * cells_coarse + span)
                vel_ref[field, :, k * fine : (k + 1) * fine] = product(
                    high[:, window], tx_ref[...]
                ) + product(low[:, window], tx_ref[...])
        acc_ref[...] = jnp.zeros_like(acc_ref)

    rate = diff_ref[level]
    row_at = lax.broadcasted_iota(jnp.int32, (rows, fine), 0)
    lane_at = lax.broadcasted_iota(jnp.int32, (rows, fine), 1)
    first_lane, last_lane = lane_at == 0, lane_at == fine - 1
    first_row, last_row = row_at == 0, row_at == rows - 1
    bottom, top = level == 0, level == last
    for k in range(chunks):
        start, stop = k * fine, (k + 1) * fine
        centre = centre_ref[0, :, start:stop]
        before = west_ref[0] if k == 0 else centre_ref[0, :, start - 1 : start]
        after = east_ref[0] if k == chunks - 1 else centre_ref[0, :, stop : stop + 1]
        west = jnp.where(first_lane, before, pltpu.roll(centre, 1, 1))
        east = jnp.where(last_lane, after, pltpu.roll(centre, fine - 1, 1))
        south = jnp.where(first_row, south_ref[0, :, start:stop], pltpu.roll(centre, 1, 0))
        north = jnp.where(
            last_row, north_ref[0, :, start:stop], pltpu.roll(centre, rows - 1, 0)
        )
        lower = jnp.where(bottom, lower_ref[0, :, start:stop], below_ref[0, :, start:stop])
        upper = jnp.where(top, upper_ref[0, :, start:stop], above_ref[0, :, start:stop])
        spread = rate * (east + west + north + south + upper + lower - 6.0 * centre)
        advection = (
            vel_ref[0, :, start:stop] * (east - west)
            + vel_ref[1, :, start:stop] * (north - south)
            + vel_ref[2, :, start:stop] * (upper - lower)
        ) * 0.5
        updated = centre + fine_step * (spread - advection)
        out_ref[0, :, start:stop] = updated
        acc_ref[:, start:stop] += vel_ref[3, :, start:stop] - updated

    @pl.when(part == RATIO - 1)
    def _():
        for k in range(chunks):
            high, low = split_parts(acc_ref[:, k * fine : (k + 1) * fine])
            half = product(ry_ref[...], high) + product(ry_ref[...], low)
            high, low = split_parts(half)
            coarse_ref[0, :, k * cells_coarse : (k + 1) * cells_coarse] = product(
                high, rx_ref[...]
            ) + product(low, rx_ref[...])


def fine_update(rimmed, salinity, halos, diffusivity):
    levels, rows, cols = salinity.shape
    fields, quarter, rim_rows, rim_cols = rimmed.shape
    row_count, width = rows // RATIO, cols // RATIO
    cells_coarse = min(128, width)
    fine = cells_coarse * RATIO
    span = cells_coarse + 128
    ty = rows_table(row_count, rim_rows)
    tx = spread_table(cells_coarse, span)
    ry = average_table(rows, 1.0 / RATIO).T
    rx = average_table(fine, 1.0 / RATIO / RATIO)

    def fixed(array):
        return pl.BlockSpec(array.shape, lambda i: (0,) * array.ndim)

    def level_block(array):
        return pl.BlockSpec((1,) + array.shape[1:], lambda i: (i, 0, 0))

    slab = (1, rows, cols)
    lower, upper, south, north, west, east = halos
    return pl.pallas_call(
        lambda *refs: step_kernel(cells_coarse, *refs),
        grid=(levels,),
        in_specs=[
            pl.BlockSpec(memory_space=pltpu.SMEM),
            pl.BlockSpec(slab, lambda i: (i, 0, 0)),
            pl.BlockSpec(slab, lambda i: (jnp.maximum(i - 1, 0), 0, 0)),
            pl.BlockSpec(slab, lambda i: (jnp.minimum(i + 1, levels - 1), 0, 0)),
            fixed(lower),
            fixed(upper),
            level_block(south),
            level_block(north),
            level_block(west),
            level_block(east),
            pl.BlockSpec((fields, 1) + rimmed.shape[2:], lambda i: (0, i // RATIO, 0, 0)),
            fixed(ty),
            fixed(tx),
            fixed(ry),
            fixed(rx),
        ],
        out_specs=[
            pl.BlockSpec(slab, lambda i: (i, 0, 0)),
            pl.BlockSpec((1, row_count, width), lambda i: (i // RATIO, 0, 0)),
        ],
        out_shape=[
            jax.ShapeDtypeStruct(salinity.shape, jnp.float32),
            jax.ShapeDtypeStruct((quarter, row_count, width), jnp.float32),
        ],
        scratch_shapes=[
            pltpu.VMEM((fields, rows, cols), jnp.float32),
            pltpu.VMEM((rows, cols), jnp.float32),
        ],
        compiler_params=pltpu.CompilerParams(
            dimension_semantics=("arbitrary",), vmem_limit_bytes=48 * 2**20
        ),
    )(
        diffusivity,
        salinity,
        salinity,
        salinity,
        lower,
        upper,
        south,
        north,
        west,
        east,
        rimmed,
        ty,
        tx,
        ry,
        rx,
    )


def side_layers(cells, axis, dim):
    count = lax.axis_size(axis)
    extent = cells.shape[dim]
    head = lax.slice_in_dim(cells, 0, 1, axis=dim)
    tail = lax.slice_in_dim(cells, extent - 1, extent, axis=dim)
    return (
        lax.ppermute(tail, axis, [(i, (i + 1) % count) for i in range(count)]),
        lax.ppermute(head, axis, [((i + 1) % count, i) for i in range(count)]),
    )


def per_device(coarse_modes, salinity, viscosity, forcing_gain, diffusivity):
    width = coarse_modes.shape[4]
    groups, columns = lax.axis_size("grp"), lax.axis_size("gx")
    halos = (
        side_layers(salinity, "grp", 0)
        + side_layers(salinity, "gy", 1)
        + side_layers(salinity, "gx", 2)
    )
    rimmed = forward(coarse_modes[0], groups, columns, lax.axis_size("gy"))
    salinity_next, restricted = fine_update(rimmed, salinity, halos, diffusivity)
    total_modes = width * columns
    mode_index = lax.axis_index("gx") * width + lax.broadcasted_iota(jnp.int32, (1, width), 1)
    wavenumber = jnp.where(mode_index < total_modes // 2, mode_index, mode_index - total_modes)
    scaled_wave = 2.0 * math.pi / total_modes * wavenumber.astype(jnp.float32)
    damping = jnp.exp(-viscosity[0] * scaled_wave * scaled_wave)
    coarse_next = backward(forcing_gain, restricted, coarse_modes[0], damping, groups, columns)
    return (salinity_next, coarse_next[None])


def solution(mesh):
    return jax.shard_map(
        per_device,
        mesh=mesh,
        in_specs=(
            P("grp", None, None, "gy", "gx"),
            P("grp", "gy", "gx"),
            P("grp"),
            P("grp"),
            P("grp"),
        ),
        out_specs=(P("grp", "gy", "gx"), P("grp", None, None, "gy", "gx")),
        check_vma=False,
    )
```

```python
import math

import jax
import jax.numpy as jnp
import numpy as np
from jax import lax
from jax.experimental import pallas as pl
from jax.experimental.pallas import tpu as pltpu
from jax.sharding import PartitionSpec as P

RATIO = 4


fine_step = 0.1


LANES = 128
SUBLANES = 8
MESH = pl.DeviceIdType.MESH


def turn_table(rows, cols, period, orient, shift):
    product = np.outer(np.arange(rows) - shift, np.arange(cols)) % period
    angle = 2.0 * np.pi / period * product
    return np.cos(angle), orient * np.sin(angle)


def twist_table(length, orient, shift):
    cosine, sine = turn_table(length // LANES, LANES, length, orient, shift)
    return (np.stack([cosine, sine]) * length ** (-0.25)).astype(np.float32)


def lane_table(length, orient, want_imag):
    tiles = length // LANES
    groups = LANES // tiles
    order = (np.arange(tiles)[None, :] * groups + np.arange(groups)[:, None]).reshape(-1)
    cosine, sine = turn_table(LANES, LANES, LANES, orient, 0)
    cosine, sine = cosine[order], sine[order]
    table = np.concatenate([cosine, -sine], axis=1)
    if want_imag:
        table = np.concatenate([table, np.concatenate([sine, cosine], axis=1)], axis=0)
    table = (table * length ** (-0.25)).astype(np.float32)
    high = table.astype(jnp.bfloat16)
    low = (table - high.astype(np.float32)).astype(jnp.bfloat16)
    return np.concatenate([high, low, high], axis=1)


def butterflies(parts, orient):
    count = len(parts)
    if count == 1:
        return parts
    even = butterflies(parts[0::2], orient)
    odd = butterflies(parts[1::2], orient)
    sums, differences = [], []
    for k in range(count // 2):
        real, imag = odd[k]
        if k == 0:
            turned = (real, imag)
        elif 4 * k == count:
            turned = (None if imag is None else -orient * imag, orient * real)
        else:
            angle = orient * 2.0 * math.pi * k / count
            cosine, sine = math.cos(angle), math.sin(angle)
            if imag is None:
                turned = (cosine * real, sine * real)
            else:
                turned = (cosine * real - sine * imag, sine * real + cosine * imag)
        first = even[k]
        sums.append((plus(first[0], turned[0]), plus(first[1], turned[1])))
        differences.append((minus(first[0], turned[0]), minus(first[1], turned[1])))
    return sums + differences


def plus(left, right):
    if left is None:
        return right
    return left if right is None else left + right


def minus(left, right):
    if right is None:
        return left
    return -right if left is None else left - right


def split_stack(value):
    high, low = split_parts(value)
    return jnp.concatenate([high, high, low], axis=1)


def transform_lines(tiles, orient, shift, twist_ref, table_ref, mid_ref):
    count = len(tiles)
    bins = butterflies(tiles, orient)
    for r in range(count):
        real, imag = bins[(r - shift) % count]
        cosine, sine = twist_ref[0, r : r + 1, :], twist_ref[1, r : r + 1, :]
        at = slice(r * SUBLANES, (r + 1) * SUBLANES)
        if imag is None:
            mid_ref[0, at, :], mid_ref[1, at, :] = real * cosine, real * sine
        else:
            mid_ref[0, at, :] = real * cosine - imag * sine
            mid_ref[1, at, :] = real * sine + imag * cosine
    parts = [
        jnp.concatenate(
            [mid_ref[k, pl.ds(row, count, stride=SUBLANES), :] for row in range(SUBLANES)], axis=0
        )
        for k in range(2)
    ]
    stacked = split_stack(jnp.concatenate(parts, axis=1))
    return lax.dot_general(
        table_ref[...], stacked, (((1,), (1,)), ((), ())), preferred_element_type=jnp.float32
    )


def natural_tiles(result, count, turn_ref):
    groups = LANES // count
    group_at = lax.broadcasted_iota(jnp.int32, (count, LANES), 1) // count
    for tile in range(SUBLANES // groups):
        lanes = slice(tile * LANES, (tile + 1) * LANES)
        pieces = [result[k * count : (k + 1) * count, lanes] for k in range(groups)]
        for row in range(groups):
            line = None
            for k in range(groups):
                shift = count * (k - row) % LANES
                moved = pieces[k] if shift == 0 else pltpu.roll(pieces[k], shift, 1)
                line = moved if line is None else jnp.where(group_at == k, moved, line)
            start = (tile * groups + row) * count
            turn_ref[start : start + count, :] = line
    return [turn_ref[pl.ds(u, SUBLANES, stride=count), :] for u in range(count)]


def greet(groups, columns, neighbours):
    barrier = pltpu.get_barrier_semaphore()
    mine, at = lax.axis_index("grp"), lax.axis_index("gx")
    total = 0
    for d in range(groups):
        for e in range(columns):
            if d == 0 and e == 0:
                continue
            pl.semaphore_signal(
                barrier,
                inc=1,
                device_id={"grp": lax.rem(mine + d, groups), "gx": lax.rem(at + e, columns)},
                device_id_type=MESH,
            )
            total += 1
    for neighbour in neighbours:
        pl.semaphore_signal(barrier, inc=1, device_id={"gy": neighbour}, device_id_type=MESH)
        total += 1
    pl.semaphore_wait(barrier, total)


def forward_kernel(
    groups,
    columns,
    halves_y,
    modes_ref,
    cells_ref,
    twist_hbm,
    table_hbm,
    rim_ref,
    heat_ref,
    edge_ref,
    south_ref,
    north_ref,
    outer_ref,
    pencil,
    mid,
    turn,
    lines,
    landed,
    side_out,
    side_in,
    twist_ref,
    table_ref,
    edge_rows,
    edge_cols,
    row_out,
    row_in,
    col_out,
    col_in,
    send_one,
    recv_one,
    own_sem,
    send_two,
    recv_two,
    side_send,
    side_recv,
    load_sem,
    row_send,
    row_recv,
    col_send,
    col_recv,
    outer_send,
    outer_recv,
):
    mine, at, half = lax.axis_index("grp"), lax.axis_index("gx"), lax.axis_index("gy")
    above, below = lax.rem(half + 1, halves_y), lax.rem(half + halves_y - 1, halves_y)
    planes, rows, width = modes_ref.shape[1:]
    quarter = planes // groups
    row_blocks = rows // SUBLANES
    blocks = quarter * row_blocks
    turns = pencil.shape[0]
    count = pencil.shape[3] // LANES
    span = width + LANES
    levels, fine_rows, fine_cols = cells_ref.shape
    loads = [
        pltpu.make_async_copy(source, target, load_sem.at[k])
        for k, (source, target) in enumerate(
            (
                (cells_ref.at[:, pl.ds(fine_rows - SUBLANES, SUBLANES), :], edge_rows.at[0]),
                (cells_ref.at[:, pl.ds(0, SUBLANES), :], edge_rows.at[1]),
                (cells_ref.at[:, :, pl.ds(fine_cols - LANES, LANES)], edge_cols.at[0]),
                (cells_ref.at[:, :, pl.ds(0, LANES)], edge_cols.at[1]),
                (twist_hbm, twist_ref),
                (table_hbm, table_ref),
            )
        )
    ]
    for load in loads:
        load.start()
    greet(groups, columns, (above, below))

    def place(block):
        group, inner = block // blocks, lax.rem(block, blocks)
        plane = inner // row_blocks
        row = pl.multiple_of(lax.rem(inner, row_blocks) * SUBLANES, SUBLANES)
        return group, inner, plane, row

    def first_copy(i, d):
        other = lax.rem(at + d, columns)
        group, _, plane, row = place(other + columns * i)
        source = modes_ref.at[:, group * quarter + plane, pl.ds(row, SUBLANES), :]
        target = pencil.at[i, :, :, pl.ds(pl.multiple_of(at * width, LANES), width)]
        if d == 0:
            return pltpu.make_async_copy(source, target, own_sem.at[i])
        return pltpu.make_async_remote_copy(
            src_ref=source,
            dst_ref=target,
            send_sem=send_one.at[i, d],
            recv_sem=recv_one.at[i, d],
            device_id={"gx": other},
            device_id_type=MESH,
        )

    def outer_copies(piece):
        row = pl.ds(piece * SUBLANES, SUBLANES)
        return [
            pltpu.make_async_remote_copy(
                src_ref=cells_ref.at[(levels - 1, 0)[k], row, :],
                dst_ref=outer_ref.at[k, row, :],
                send_sem=outer_send.at[k, piece],
                recv_sem=outer_recv.at[k, piece],
                device_id={"grp": lax.rem(mine + (1, groups - 1)[k], groups)},
                device_id_type=MESH,
            )
            for k in range(2)
        ]

    pieces = fine_rows // SUBLANES
    ahead = min(4, pieces)
    during = min(turns, pieces - ahead)

    def start_outer(piece):
        for copy in outer_copies(piece):
            copy.start()

    for i in range(turns):
        for d in range(columns):
            first_copy(i, (d + 1) % columns).start()
    for piece in range(ahead):
        start_outer(piece)

    for load in loads:
        load.wait()
    lane_at = lax.broadcasted_iota(jnp.int32, (fine_rows, LANES), 1)
    for level in range(levels):
        row_out[0, level : level + 1, :] = edge_rows[0, level, SUBLANES - 1 : SUBLANES, :]
        row_out[1, level : level + 1, :] = edge_rows[1, level, 0:1, :]
    for k in range(2):
        packed = jnp.zeros((fine_rows, LANES), jnp.float32)
        for level in range(levels):
            column = edge_cols[k, level, :, LANES - 1 : LANES] if k == 0 else edge_cols[k, level, :, 0:1]
            packed = jnp.where(lane_at == level, column, packed)
        col_out[k] = packed
    outer = []
    for k in range(2):
        outer.append(
            pltpu.make_async_remote_copy(
                src_ref=row_out.at[k],
                dst_ref=row_in.at[k],
                send_sem=row_send.at[k],
                recv_sem=row_recv.at[k],
                device_id={"gy": (above, below)[k]},
                device_id_type=MESH,
            )
        )
        outer.append(
            pltpu.make_async_remote_copy(
                src_ref=col_out.at[k],
                dst_ref=col_in.at[k],
                send_sem=col_send.at[k],
                recv_sem=col_recv.at[k],
                device_id={"gx": lax.rem(at + (1, columns - 1)[k], columns)},
                device_id_type=MESH,
            )
        )
    for copy in outer:
        copy.start()

    def second_copy(i, b):
        group, inner, plane, row = place(at + columns * i)
        source = lines.at[i, :, pl.ds(b * width, span)]
        target = landed.at[mine, plane, pl.ds(row, SUBLANES), :]
        remote = lambda: pltpu.make_async_remote_copy(
            src_ref=source,
            dst_ref=target,
            send_sem=send_two.at[i, b],
            recv_sem=recv_two.at[mine, inner],
            device_id={"grp": group, "gx": b},
            device_id_type=MESH,
        )
        local = lambda: pltpu.make_async_copy(source, target, recv_two.at[mine, inner])
        stays = jnp.logical_and(group == mine, at == b)
        return remote, local, stays

    def one_turn(i, carry):
        for d in range(columns):
            if d == 0:
                first_copy(i, 0).wait()
            else:
                first_copy(i, d).wait_recv()
        tiles = [
            tuple(pencil[i, k, :, p * LANES : (p + 1) * LANES] for k in range(2))
            for p in range(count)
        ]
        result = transform_lines(tiles, 1.0, 1, twist_ref, table_ref, mid)
        for u, tile in enumerate(natural_tiles(result, count, turn)):
            lines[i, :, u * LANES : (u + 1) * LANES] = tile
            if u == 0:
                lines[i, :, count * LANES : (count + 1) * LANES] = tile
        for b in range(columns):
            remote, local, stays = second_copy(i, b)
            pl.when(stays)(lambda: local().start())
            pl.when(jnp.logical_not(stays))(lambda: remote().start())
        if during == turns:
            start_outer(ahead + i)
        else:
            pl.when(i < during)(lambda: start_outer(ahead + i))
        return carry

    lax.fori_loop(0, turns, one_turn, 0)
    for piece in range(ahead + during, pieces):
        start_outer(piece)
    for field in range(groups):
        for inner in range(blocks):
            plane, row = inner // row_blocks, inner % row_blocks * SUBLANES
            target = landed.at[field, plane, pl.ds(row, SUBLANES), :]
            pltpu.make_async_copy(target, target, recv_two.at[field, inner]).wait()
    for field in range(groups):
        for plane in range(quarter):
            k = field * quarter + plane
            side_out[0, k : k + 1, :] = landed[field, plane, rows - 1 : rows, :]
            side_out[1, k : k + 1, :] = landed[field, plane, 0:1, :]
    sides = [
        pltpu.make_async_remote_copy(
            src_ref=side_out.at[k],
            dst_ref=side_in.at[k],
            send_sem=side_send.at[k],
            recv_sem=side_recv.at[k],
            device_id={"gy": (above, below)[k]},
            device_id_type=MESH,
        )
        for k in range(2)
    ]
    for side in sides:
        side.start()
    scale = fine_step * 0.5
    for field in range(groups - 1):
        for plane in range(quarter):
            rim_ref[field, plane, 0:rows, :] = scale * landed[field, plane]
    for copy in outer:
        copy.wait()
    for level in range(levels):
        south_ref[level] = row_in[0, level : level + 1, :]
        north_ref[level] = row_in[1, level : level + 1, :]
        edge_ref[level] = jnp.where(
            lane_at < LANES // 2,
            col_in[1, :, level : level + 1],
            col_in[0, :, level : level + 1],
        )
    for side in sides:
        side.wait()
    rest = rim_ref.shape[2] - rows - 2
    for field in range(groups - 1):
        for plane in range(quarter):
            k = field * quarter + plane
            tail = jnp.concatenate(
                [
                    scale * side_in[0, k : k + 1, :],
                    scale * side_in[1, k : k + 1, :],
                    jnp.zeros((rest, span), jnp.float32),
                ],
                axis=0,
            )
            rim_ref[field, plane, rows:, :] = tail
    near, far = mean_weights()
    row_at = lax.broadcasted_iota(jnp.int32, (rows, span), 0)
    for plane in range(quarter):
        k = (groups - 1) * quarter + plane
        heat = landed[groups - 1, plane]
        before = jnp.where(row_at == 0, side_in[0, k : k + 1, :], pltpu.roll(heat, 1, 0))
        after = jnp.where(row_at == rows - 1, side_in[1, k : k + 1, :], pltpu.roll(heat, rows - 1, 0))
        heat = near * heat + far * (before + after)
        heat = near * pltpu.roll(heat, span - 1, 1) + far * (heat + pltpu.roll(heat, span - 2, 1))
        heat_ref[plane] = heat[:, :width]
    for piece in range(pieces):
        for copy in outer_copies(piece):
            copy.wait()
    for i in range(turns):
        for d in range(1, columns):
            first_copy(i, d).wait_send()
        for b in range(columns):
            remote, _, stays = second_copy(i, b)
            pl.when(jnp.logical_not(stays))(lambda: remote().wait_send())


def mean_weights():
    offsets = [(s + 0.5) / RATIO - 0.5 for s in range(RATIO)]
    near = sum(1.0 - abs(offset) for offset in offsets) / RATIO
    return near, (1.0 - near) / 2.0


def forward(modes, cells, groups, columns, halves_y):
    _, planes, rows, width = modes.shape
    levels, fine_rows, fine_cols = cells.shape
    length = width * columns
    quarter = planes // groups
    blocks = quarter * (rows // SUBLANES)
    turns = groups * blocks // columns
    count = length // LANES
    span = width + LANES
    deep = -(-(rows + 2) // 16) * 16
    twist = twist_table(length, 1.0, 1)
    table = lane_table(length, 1.0, False)
    vmem = pl.BlockSpec(memory_space=pltpu.VMEM)
    dma = pltpu.SemaphoreType.DMA
    return pl.pallas_call(
        lambda *refs: forward_kernel(groups, columns, halves_y, *refs),
        name="forward_lines",
        out_shape=[
            jax.ShapeDtypeStruct((groups - 1, quarter, deep, span), jnp.float32),
            jax.ShapeDtypeStruct((quarter, rows, width), jnp.float32),
            jax.ShapeDtypeStruct((levels, fine_rows, LANES), jnp.float32),
            jax.ShapeDtypeStruct((levels, 1, fine_cols), jnp.float32),
            jax.ShapeDtypeStruct((levels, 1, fine_cols), jnp.float32),
            jax.ShapeDtypeStruct((2, fine_rows, fine_cols), jnp.float32),
        ],
        in_specs=[pl.BlockSpec(memory_space=pltpu.HBM)] * 4,
        out_specs=[vmem] * 5 + [pl.BlockSpec(memory_space=pltpu.HBM)],
        scratch_shapes=[
            pltpu.VMEM((turns, 2, SUBLANES, length), jnp.float32),
            pltpu.VMEM((2, SUBLANES * count, LANES), jnp.float32),
            pltpu.VMEM((SUBLANES * count, LANES), jnp.float32),
            pltpu.VMEM((turns, SUBLANES, length + LANES), jnp.float32),
            pltpu.VMEM((groups, quarter, rows, span), jnp.float32),
            pltpu.VMEM((2, groups * quarter, span), jnp.float32),
            pltpu.VMEM((2, groups * quarter, span), jnp.float32),
            pltpu.VMEM(twist.shape, jnp.float32),
            pltpu.VMEM(table.shape, jnp.bfloat16),
            pltpu.VMEM((2, levels, SUBLANES, fine_cols), jnp.float32),
            pltpu.VMEM((2, levels, fine_rows, LANES), jnp.float32),
            pltpu.VMEM((2, levels, fine_cols), jnp.float32),
            pltpu.VMEM((2, levels, fine_cols), jnp.float32),
            pltpu.VMEM((2, fine_rows, LANES), jnp.float32),
            pltpu.VMEM((2, fine_rows, LANES), jnp.float32),
            dma((turns, columns)),
            dma((turns, columns)),
            dma((turns,)),
            dma((turns, columns)),
            dma((groups, blocks)),
            dma((2,)),
            dma((2,)),
            dma((6,)),
            dma((2,)),
            dma((2,)),
            dma((2,)),
            dma((2,)),
            dma((2, fine_rows // SUBLANES)),
            dma((2, fine_rows // SUBLANES)),
        ],
        compiler_params=pltpu.CompilerParams(
            collective_id=0, has_side_effects=True, vmem_limit_bytes=63 * 2**20
        ),
        cost_estimate=pl.CostEstimate(flops=10**9, bytes_accessed=10**8, transcendentals=0),
    )(modes, cells, twist, table)


def backward_kernel(
    groups,
    columns,
    rates_ref,
    cells_ref,
    modes_ref,
    damp_ref,
    twist_ref,
    table_ref,
    out_ref,
    pencil,
    mid,
    turn,
    lines,
    spectrum,
    send_one,
    recv_one,
    send_two,
    recv_two,
    send_three,
):
    mine, at = lax.axis_index("grp"), lax.axis_index("gx")
    planes, rows, width = modes_ref.shape[1:]
    quarter = planes // groups
    row_blocks = rows // SUBLANES
    blocks = quarter * row_blocks
    slots = pencil.shape[0]
    count = pencil.shape[2] // LANES
    greet(groups, columns, ())

    def where_is(block):
        return block // row_blocks, block % row_blocks * SUBLANES

    def to_worker(block):
        worker, slot = block % columns, block // columns
        plane, row = where_is(block)
        source = cells_ref.at[plane, pl.ds(row, SUBLANES), :]
        target = pencil.at[slot, :, pl.ds(pl.multiple_of(at * width, LANES), width)]
        remote = lambda: pltpu.make_async_remote_copy(
            src_ref=source,
            dst_ref=target,
            send_sem=send_one.at[block],
            recv_sem=recv_one.at[slot, at],
            device_id={"gx": worker},
            device_id_type=MESH,
        )
        local = lambda: pltpu.make_async_copy(source, target, recv_one.at[slot, at])
        return remote, local, at == worker

    for block in range(blocks):
        remote, local, stays = to_worker(block)
        pl.when(stays)(lambda: local().start())
        pl.when(jnp.logical_not(stays))(lambda: remote().start())

    def to_owner(slot, b):
        block = at + columns * slot
        plane, row = block // row_blocks, lax.rem(block, row_blocks) * SUBLANES
        row = pl.multiple_of(row, SUBLANES)
        source = lines.at[slot, :, :, pl.ds(b * width, width)]
        target = spectrum.at[:, mine * quarter + plane, pl.ds(row, SUBLANES), :]
        remote = lambda: pltpu.make_async_remote_copy(
            src_ref=source,
            dst_ref=target,
            send_sem=send_two.at[slot, b],
            recv_sem=recv_two.at[mine, block],
            device_id={"gx": b},
            device_id_type=MESH,
        )
        local = lambda: pltpu.make_async_copy(source, target, recv_two.at[mine, block])
        return remote, local, at == b

    for slot in range(slots):

        def work(slot=slot):
            for e in range(columns):
                target = pencil.at[slot, :, pl.ds(e * width, width)]
                pltpu.make_async_copy(target, target, recv_one.at[slot, e]).wait()
            tiles = [(pencil[slot, :, u * LANES : (u + 1) * LANES], None) for u in range(count)]
            result = transform_lines(tiles, -1.0, 0, twist_ref, table_ref, mid)
            for k in range(2):
                part = result[k * LANES : (k + 1) * LANES]
                for u, tile in enumerate(natural_tiles(part, count, turn)):
                    lines[slot, k, :, u * LANES : (u + 1) * LANES] = tile
            for b in range(columns):
                remote, local, stays = to_owner(slot, b)
                pl.when(stays)(lambda: local().start())
                pl.when(jnp.logical_not(stays))(lambda: remote().start())

        if blocks % columns == 0:
            work()
        else:
            pl.when(at + columns * slot < blocks)(work)

    def arrival(group, block):
        plane, row = where_is(block)
        target = spectrum.at[:, group * quarter + plane, pl.ds(row, SUBLANES), :]
        return pltpu.make_async_copy(target, target, recv_two.at[group, block])

    def onward(block, d):
        plane, row = where_is(block)
        target = spectrum.at[:, mine * quarter + plane, pl.ds(row, SUBLANES), :]
        return pltpu.make_async_remote_copy(
            src_ref=target,
            dst_ref=target,
            send_sem=send_three.at[block, d],
            recv_sem=recv_two.at[mine, block],
            device_id={"grp": lax.rem(mine + d, groups)},
            device_id_type=MESH,
        )

    def finish(group, block):
        plane, row = where_is(block)
        index = group * quarter + plane
        for k in range(2):
            at_rows = pl.ds(row, SUBLANES)
            out_ref[k, index, at_rows, :] = (
                damp_ref[...] * modes_ref[k, index, at_rows, :]
                + rates_ref[0] * spectrum[k, index, at_rows, :]
            )

    for block in range(blocks):
        arrival(mine, block).wait()
        for d in range(1, groups):
            onward(block, d).start()
    for block in range(blocks):
        finish(mine, block)
    for block in range(blocks):
        for d in range(1, groups):
            group = lax.rem(mine + d, groups)
            arrival(group, block).wait()
            finish(group, block)
    for block in range(blocks):
        remote, _, stays = to_worker(block)
        pl.when(jnp.logical_not(stays))(lambda: remote().wait_send())
        for d in range(1, groups):
            onward(block, d).wait_send()
    for slot in range(slots):
        for b in range(columns):
            remote, _, stays = to_owner(slot, b)
            sent = jnp.logical_not(stays)
            if blocks % columns:
                sent = jnp.logical_and(sent, at + columns * slot < blocks)
            pl.when(sent)(lambda: remote().wait_send())


def backward(gain, cells, modes, damping, groups, columns):
    _, planes, rows, width = modes.shape
    length = width * columns
    quarter = planes // groups
    blocks = quarter * (rows // SUBLANES)
    slots = -(-blocks // columns)
    count = length // LANES
    twist = twist_table(length, -1.0, 0)
    table = lane_table(length, -1.0, True)
    vmem = pl.BlockSpec(memory_space=pltpu.VMEM)
    dma = pltpu.SemaphoreType.DMA
    return pl.pallas_call(
        lambda *refs: backward_kernel(groups, columns, *refs),
        name="backward_lines",
        out_shape=jax.ShapeDtypeStruct(modes.shape, jnp.float32),
        in_specs=[pl.BlockSpec(memory_space=pltpu.SMEM)] + [vmem] * 5,
        out_specs=vmem,
        scratch_shapes=[
            pltpu.VMEM((slots, SUBLANES, length), jnp.float32),
            pltpu.VMEM((2, SUBLANES * count, LANES), jnp.float32),
            pltpu.VMEM((SUBLANES * count, LANES), jnp.float32),
            pltpu.VMEM((slots, 2, SUBLANES, length), jnp.float32),
            pltpu.VMEM(modes.shape, jnp.float32),
            dma((blocks,)),
            dma((slots, columns)),
            dma((slots, columns)),
            dma((groups, blocks)),
            dma((blocks, groups)),
        ],
        compiler_params=pltpu.CompilerParams(
            collective_id=1, has_side_effects=True, vmem_limit_bytes=32 * 2**20
        ),
        cost_estimate=pl.CostEstimate(flops=10**9, bytes_accessed=5 * 10**7, transcendentals=0),
    )(gain, cells, modes, damping, twist, table)


def rows_table(row_count, source_count):
    fine_row = np.arange(row_count * RATIO)
    parent = fine_row // RATIO
    offset = (fine_row % RATIO + 0.5) / RATIO - 0.5
    table = np.zeros((row_count * RATIO, source_count), np.float32)
    beside = np.where(
        offset > 0,
        np.where(parent == row_count - 1, row_count + 1, parent + 1),
        np.where(parent == 0, row_count, parent - 1),
    )
    table[fine_row, parent] = 1.0 - np.abs(offset)
    table[fine_row, beside] = np.abs(offset)
    return np.concatenate([table, table], axis=1).astype(jnp.bfloat16)


def lanes_table(cell_count):
    fine_cell = np.arange(cell_count * RATIO)
    parent = fine_cell // RATIO
    offset = (fine_cell % RATIO + 0.5) / RATIO - 0.5
    table = np.zeros((LANES, cell_count * RATIO), np.float32)
    table[parent + 1, fine_cell] = 1.0 - np.abs(offset)
    table[np.where(offset > 0, parent + 2, parent), fine_cell] = np.abs(offset)
    return np.concatenate([table, table], axis=0).astype(jnp.bfloat16)


def average_table(fine_count, weight):
    cell = np.arange(fine_count // RATIO)[None, :]
    table = np.where(np.arange(fine_count)[:, None] // RATIO == cell, weight, 0.0)
    return np.concatenate([table, table], axis=0).astype(jnp.bfloat16)


def split_parts(value):
    high = value.astype(jnp.bfloat16)
    return high, (value - high.astype(jnp.float32)).astype(jnp.bfloat16)


def product(left, right):
    return jnp.dot(left, right, preferred_element_type=jnp.float32)


def split_pair(value, axis):
    return jnp.concatenate(split_parts(value), axis=axis)


def block_means(total, rows_ref, lanes_ref):
    half = product(rows_ref[...], split_pair(total, 0))
    fine = LANES * RATIO
    chunks = half.shape[1] // fine
    stacked = jnp.concatenate([half[:, k * fine : (k + 1) * fine] for k in range(chunks)], axis=0)
    cells = product(split_pair(stacked, 1), lanes_ref[...])
    height = half.shape[0]
    return [cells[k * height : (k + 1) * height] for k in range(chunks)]


def fine_kernel(
    rate_ref,
    cells_hbm,
    edge_ref,
    south_ref,
    north_ref,
    beyond_hbm,
    rim_ref,
    heat_ref,
    ty_ref,
    tx_ref,
    ry_ref,
    rx_ref,
    out_hbm,
    coarse_ref,
    held,
    vel,
    acc,
    ready,
    in_sem,
    out_sem,
):
    plane = pl.program_id(0)
    slabs, spans, tall = held.shape[:3]
    levels, rows, cols = cells_hbm.shape
    strips, tiles = rows // SUBLANES, cols // LANES
    fields = rim_ref.shape[0]
    pieces = vel.shape[0]
    half = LANES // 2

    def load(source, index, tile, slab):
        return pltpu.make_async_copy(
            source.at[index, :, pl.ds(pl.multiple_of(tile * LANES, LANES), LANES)],
            held.at[slab, tile, pl.ds(SUBLANES, rows), :],
            in_sem.at[slab],
        )

    def start_slab(source, index, slab):
        @pl.loop(0, tiles)
        def _(tile):
            load(source, index, tile, slab).start()

    def wait_slab(slab):
        whole = held.at[slab, pl.ds(0, tiles), pl.ds(SUBLANES, rows), :]
        pltpu.make_async_copy(whole, whole, in_sem.at[slab]).wait()

    @pl.when(plane == 0)
    def _():
        start_slab(beyond_hbm, 0, 0)

        @pl.loop(0, levels)
        def _(level):
            start_slab(cells_hbm, level, level + 1)

        start_slab(beyond_hbm, 1, slabs - 1)

    for part in range(RATIO):
        level = plane * RATIO + part
        held[level + 1, tiles, SUBLANES : SUBLANES + rows, :] = edge_ref[part]
        for tile in range(tiles):
            lanes = slice(tile * LANES, (tile + 1) * LANES)
            held[level + 1, tile, SUBLANES - 1 : SUBLANES, :] = south_ref[part, :, lanes]
            held[level + 1, tile, SUBLANES + rows : SUBLANES + rows + 1, :] = north_ref[part, :, lanes]

    along = jnp.concatenate(
        [product(ty_ref[...], split_pair(rim_ref[field, 0], 0)) for field in range(fields)],
        axis=0,
    )
    span = along.shape[1]
    views = [split_parts(along), split_parts(pltpu.roll(along, span - half, 1))]
    group = min(4, pieces)
    for first in range(0, pieces, group):
        windows = []
        for k in range(first, first + group):
            high, low = views[k % 2]
            lanes = slice(k // 2 * LANES, (k // 2 + 1) * LANES)
            windows.append(jnp.concatenate([high[:, lanes], low[:, lanes]], axis=1))
        refined = product(jnp.concatenate(windows, axis=0), tx_ref[...])
        for k in range(group):
            vel[first + k] = refined[k * fields * rows : (k + 1) * fields * rows]

    @pl.when(plane == 0)
    def _():
        wait_slab(0)
        wait_slab(1)

    for part in range(RATIO):
        wait_slab(plane * RATIO + part + 2)

    side_rates = [fine_step * rate_ref[plane * RATIO + part] for part in range(RATIO)]
    own_rates = [1.0 - 6.0 * rate for rate in side_rates]
    lane_at = lax.broadcasted_iota(jnp.int32, (SUBLANES, LANES), 1)
    first_lane, last_lane = lane_at == 0, lane_at == LANES - 1
    per_turn = vel.shape[2] // LANES
    base = plane * RATIO

    def out_copy(index, strip):
        at = pl.ds(pl.multiple_of(strip * SUBLANES, SUBLANES), SUBLANES)
        block = pl.ds(index * RATIO, RATIO)
        return pltpu.make_async_copy(
            ready.at[block, at, :], out_hbm.at[block, at, :], out_sem.at[index, strip]
        )

    @pl.loop(0, strips)
    def _(s):
        start = pl.multiple_of(s * SUBLANES, SUBLANES)
        at = pl.ds(start, SUBLANES)
        middle = pl.ds(start + SUBLANES, SUBLANES)
        below, above = pl.ds(start + SUBLANES - 1, SUBLANES), pl.ds(start + SUBLANES + 1, SUBLANES)
        slabs_here = [base + part + 1 for part in range(RATIO)]
        west_turned = [pltpu.roll(held[slab, tiles, middle, :], 1, 1) for slab in slabs_here]
        centre = [held[slab, 0, middle, :] for slab in slabs_here]
        east_turned = [pltpu.roll(x, LANES - 1, 1) for x in centre]
        for tile in range(tiles):
            k, j = divmod(tile, per_turn)
            lanes = slice(tile * LANES, (tile + 1) * LANES)
            inner = slice(j * LANES, (j + 1) * LANES)
            ahead = [held[slab, tile + 1, middle, :] for slab in slabs_here]
            ahead_turned = [pltpu.roll(x, LANES - 1, 1) for x in ahead]
            here_turned = [pltpu.roll(x, 1, 1) for x in centre]
            column = (
                [held[base, tile, middle, :]] + centre + [held[base + RATIO + 1, tile, middle, :]]
            )
            flow = [
                vel[k, pl.ds(pl.multiple_of(f * rows + start, SUBLANES), SUBLANES), inner]
                for f in range(fields)
            ]
            total = None
            for part, slab in enumerate(slabs_here):
                west = jnp.where(first_lane, west_turned[part], here_turned[part])
                east = jnp.where(last_lane, ahead_turned[part], east_turned[part])
                south, north = held[slab, tile, below, :], held[slab, tile, above, :]
                lower, upper = column[part], column[part + 2]
                around = (east + west) + (north + south) + (upper + lower)
                advection = (
                    flow[0] * (east - west)
                    + flow[1] * (north - south)
                    + flow[2] * (upper - lower)
                )
                updated = own_rates[part] * centre[part] + side_rates[part] * around - advection
                ready[base + part, at, lanes] = updated
                total = updated if total is None else total + updated
            acc[at, lanes] = total
            west_turned, centre, east_turned = here_turned, ahead, ahead_turned
        out_copy(plane, s).start()

    for k, cells in enumerate(block_means(acc[...], ry_ref, rx_ref)):
        lanes = slice(k * LANES, (k + 1) * LANES)
        coarse_ref[0, :, lanes] = heat_ref[0, :, lanes] - cells

    @pl.when(plane == pl.num_programs(0) - 1)
    def _():
        for index in range(levels // RATIO):
            for s in range(strips):
                out_copy(index, s).wait()


def fine_update(rimmed, heat, edge, south, north, beyond, salinity, diffusivity):
    levels, rows, cols = salinity.shape
    fields, quarter = rimmed.shape[:2]
    row_count, width = rows // RATIO, cols // RATIO
    cell_count = LANES // 2
    ty = rows_table(row_count, rimmed.shape[2])
    tx = lanes_table(cell_count)
    ry = average_table(rows, 1.0 / RATIO).T
    rx = average_table(LANES * RATIO, 1.0 / RATIO / RATIO)
    pieces = width // cell_count

    def fixed(array):
        return pl.BlockSpec(array.shape, lambda i: (0,) * array.ndim)

    hbm = pl.BlockSpec(memory_space=pltpu.HBM)
    return pl.pallas_call(
        fine_kernel,
        name="fine_levels",
        grid=(quarter,),
        in_specs=[
            pl.BlockSpec(memory_space=pltpu.SMEM),
            hbm,
            pl.BlockSpec((RATIO, rows, LANES), lambda i: (i, 0, 0)),
            pl.BlockSpec((RATIO, 1, cols), lambda i: (i, 0, 0)),
            pl.BlockSpec((RATIO, 1, cols), lambda i: (i, 0, 0)),
            hbm,
            pl.BlockSpec((fields, 1) + rimmed.shape[2:], lambda i: (0, i, 0, 0)),
            pl.BlockSpec((1, row_count, width), lambda i: (i, 0, 0)),
            fixed(ty),
            fixed(tx),
            fixed(ry),
            fixed(rx),
        ],
        out_specs=[hbm, pl.BlockSpec((1, row_count, width), lambda i: (i, 0, 0))],
        out_shape=[
            jax.ShapeDtypeStruct(salinity.shape, jnp.float32),
            jax.ShapeDtypeStruct((quarter, row_count, width), jnp.float32),
        ],
        scratch_shapes=[
            pltpu.VMEM((levels + 2, cols // LANES + 1, rows + 2 * SUBLANES, LANES), jnp.float32),
            pltpu.VMEM((pieces, fields * rows, cell_count * RATIO), jnp.float32),
            pltpu.VMEM((rows, cols), jnp.float32),
            pltpu.VMEM((levels, rows, cols), jnp.float32),
            pltpu.SemaphoreType.DMA((levels + 2,)),
            pltpu.SemaphoreType.DMA((quarter, rows // SUBLANES)),
        ],
        compiler_params=pltpu.CompilerParams(
            dimension_semantics=("arbitrary",), vmem_limit_bytes=63 * 2**20
        ),
        cost_estimate=pl.CostEstimate(flops=10**9, bytes_accessed=4 * 10**7, transcendentals=0),
    )(diffusivity, salinity, edge, south, north, beyond, rimmed, heat, ty, tx, ry, rx)


def per_device(coarse_modes, salinity, viscosity, forcing_gain, diffusivity):
    width = coarse_modes.shape[4]
    groups, columns = lax.axis_size("grp"), lax.axis_size("gx")
    rimmed, heat, edge, south, north, beyond = forward(
        coarse_modes[0], salinity, groups, columns, lax.axis_size("gy")
    )
    salinity_next, restricted = fine_update(
        rimmed, heat, edge, south, north, beyond, salinity, diffusivity
    )
    total_modes = width * columns
    mode_index = lax.axis_index("gx") * width + lax.broadcasted_iota(jnp.int32, (1, width), 1)
    wavenumber = jnp.where(mode_index < total_modes // 2, mode_index, mode_index - total_modes)
    scaled_wave = 2.0 * math.pi / total_modes * wavenumber.astype(jnp.float32)
    damping = jnp.exp(-viscosity[0] * scaled_wave * scaled_wave)
    coarse_next = backward(forcing_gain, restricted, coarse_modes[0], damping, groups, columns)
    return (salinity_next, coarse_next[None])


def solution(mesh):
    return jax.shard_map(
        per_device,
        mesh=mesh,
        in_specs=(
            P("grp", None, None, "gy", "gx"),
            P("grp", "gy", "gx"),
            P("grp"),
            P("grp"),
            P("grp"),
        ),
        out_specs=(P("grp", "gy", "gx"), P("grp", None, None, "gy", "gx")),
        check_vma=False,
    )
```

```python
import math

import jax
import jax.numpy as jnp
import numpy as np
from jax import lax
from jax.experimental import pallas as pl
from jax.experimental.pallas import tpu as pltpu
from jax.sharding import PartitionSpec as P

RATIO = 4
LATE_PIECES = 6


fine_step = 0.1


LANES = 128
SUBLANES = 8
MESH = pl.DeviceIdType.MESH


def turn_table(rows, cols, period, orient, shift):
    product = np.outer(np.arange(rows) - shift, np.arange(cols)) % period
    angle = 2.0 * np.pi / period * product
    return np.cos(angle), orient * np.sin(angle)


def twist_table(length, orient, shift):
    cosine, sine = turn_table(length // LANES, LANES, length, orient, shift)
    return (np.stack([cosine, sine]) * length ** (-0.25)).astype(np.float32)


def lane_table(length, orient, want_imag):
    tiles = length // LANES
    groups = LANES // tiles
    order = (np.arange(tiles)[None, :] * groups + np.arange(groups)[:, None]).reshape(-1)
    cosine, sine = turn_table(LANES, LANES, LANES, orient, 0)
    cosine, sine = cosine[order], sine[order]
    table = np.concatenate([cosine, -sine], axis=1)
    if want_imag:
        table = np.concatenate([table, np.concatenate([sine, cosine], axis=1)], axis=0)
    table = (table * length ** (-0.25)).astype(np.float32)
    high = table.astype(jnp.bfloat16)
    low = (table - high.astype(np.float32)).astype(jnp.bfloat16)
    return np.concatenate([high, low, high], axis=1)


def butterflies(parts, orient):
    count = len(parts)
    if count == 1:
        return parts
    even = butterflies(parts[0::2], orient)
    odd = butterflies(parts[1::2], orient)
    sums, differences = [], []
    for k in range(count // 2):
        real, imag = odd[k]
        if k == 0:
            turned = (real, imag)
        elif 4 * k == count:
            turned = (None if imag is None else -orient * imag, orient * real)
        else:
            angle = orient * 2.0 * math.pi * k / count
            cosine, sine = math.cos(angle), math.sin(angle)
            if imag is None:
                turned = (cosine * real, sine * real)
            else:
                turned = (cosine * real - sine * imag, sine * real + cosine * imag)
        first = even[k]
        sums.append((plus(first[0], turned[0]), plus(first[1], turned[1])))
        differences.append((minus(first[0], turned[0]), minus(first[1], turned[1])))
    return sums + differences


def plus(left, right):
    if left is None:
        return right
    return left if right is None else left + right


def minus(left, right):
    if right is None:
        return left
    return -right if left is None else left - right


def split_stack(value):
    high, low = split_parts(value)
    return jnp.concatenate([high, high, low], axis=1)


def transform_lines(tiles, orient, shift, twist_ref, table_ref, mid_ref):
    count = len(tiles)
    bins = butterflies(tiles, orient)
    for r in range(count):
        real, imag = bins[(r - shift) % count]
        cosine, sine = twist_ref[0, r : r + 1, :], twist_ref[1, r : r + 1, :]
        at = slice(r * SUBLANES, (r + 1) * SUBLANES)
        if imag is None:
            mid_ref[0, at, :], mid_ref[1, at, :] = real * cosine, real * sine
        else:
            mid_ref[0, at, :] = real * cosine - imag * sine
            mid_ref[1, at, :] = real * sine + imag * cosine
    parts = [
        jnp.concatenate(
            [mid_ref[k, pl.ds(row, count, stride=SUBLANES), :] for row in range(SUBLANES)], axis=0
        )
        for k in range(2)
    ]
    stacked = split_stack(jnp.concatenate(parts, axis=1))
    return lax.dot_general(
        table_ref[...], stacked, (((1,), (1,)), ((), ())), preferred_element_type=jnp.float32
    )


def natural_tiles(result, count, turn_ref):
    groups = LANES // count
    group_at = lax.broadcasted_iota(jnp.int32, (count, LANES), 1) // count
    for tile in range(SUBLANES // groups):
        lanes = slice(tile * LANES, (tile + 1) * LANES)
        pieces = [result[k * count : (k + 1) * count, lanes] for k in range(groups)]
        for row in range(groups):
            line = None
            for k in range(groups):
                shift = count * (k - row) % LANES
                moved = pieces[k] if shift == 0 else pltpu.roll(pieces[k], shift, 1)
                line = moved if line is None else jnp.where(group_at == k, moved, line)
            start = (tile * groups + row) * count
            turn_ref[start : start + count, :] = line
    return [turn_ref[pl.ds(u, SUBLANES, stride=count), :] for u in range(count)]


def greet(groups, columns, neighbours):
    barrier = pltpu.get_barrier_semaphore()
    mine, at = lax.axis_index("grp"), lax.axis_index("gx")
    total = 0
    for d in range(groups):
        for e in range(columns):
            if d == 0 and e == 0:
                continue
            pl.semaphore_signal(
                barrier,
                inc=1,
                device_id={"grp": lax.rem(mine + d, groups), "gx": lax.rem(at + e, columns)},
                device_id_type=MESH,
            )
            total += 1
    for neighbour in neighbours:
        pl.semaphore_signal(barrier, inc=1, device_id={"gy": neighbour}, device_id_type=MESH)
        total += 1
    pl.semaphore_wait(barrier, total)


def forward_kernel(
    groups,
    columns,
    halves_y,
    modes_ref,
    cells_ref,
    twist_hbm,
    table_hbm,
    rim_ref,
    heat_ref,
    edge_ref,
    south_ref,
    north_ref,
    under_ref,
    over_ref,
    low_ref,
    pencil,
    mid,
    turn,
    lines,
    landed,
    side_out,
    side_in,
    twist_ref,
    table_ref,
    edge_rows,
    edge_cols,
    row_out,
    row_in,
    col_out,
    col_in,
    send_one,
    recv_one,
    own_sem,
    send_two,
    recv_two,
    side_send,
    side_recv,
    load_sem,
    row_send,
    row_recv,
    col_send,
    col_recv,
    outer_send,
    outer_recv,
    late,
    late_sem,
):
    mine, at, half = lax.axis_index("grp"), lax.axis_index("gx"), lax.axis_index("gy")
    above, below = lax.rem(half + 1, halves_y), lax.rem(half + halves_y - 1, halves_y)
    planes, rows, width = modes_ref.shape[1:]
    quarter = planes // groups
    row_blocks = rows // SUBLANES
    blocks = quarter * row_blocks
    turns = pencil.shape[0]
    count = pencil.shape[3] // LANES
    span = width + LANES
    levels, fine_rows, fine_cols = cells_ref.shape
    loads = [
        pltpu.make_async_copy(source, target, load_sem.at[k])
        for k, (source, target) in enumerate(
            (
                (cells_ref.at[:, pl.ds(fine_rows - SUBLANES, SUBLANES), :], edge_rows.at[0]),
                (cells_ref.at[:, pl.ds(0, SUBLANES), :], edge_rows.at[1]),
                (cells_ref.at[:, :, pl.ds(fine_cols - LANES, LANES)], edge_cols.at[0]),
                (cells_ref.at[:, :, pl.ds(0, LANES)], edge_cols.at[1]),
                (twist_hbm, twist_ref),
                (table_hbm, table_ref),
            )
        )
    ]
    early_rows = over_ref.shape[1]
    late_rows = pl.ds(early_rows, fine_rows - early_rows)
    late_in = pltpu.make_async_copy(cells_ref.at[0, late_rows, :], late, late_sem.at[0])
    late_out = pltpu.make_async_copy(late, low_ref.at[0], late_sem.at[1])
    for load in loads + [late_in]:
        load.start()
    greet(groups, columns, (above, below))

    def place(block):
        group, inner = block // blocks, lax.rem(block, blocks)
        plane = inner // row_blocks
        row = pl.multiple_of(lax.rem(inner, row_blocks) * SUBLANES, SUBLANES)
        return group, inner, plane, row

    def first_copy(i, d):
        other = lax.rem(at + d, columns)
        group, _, plane, row = place(other + columns * i)
        source = modes_ref.at[:, group * quarter + plane, pl.ds(row, SUBLANES), :]
        target = pencil.at[i, :, :, pl.ds(pl.multiple_of(at * width, LANES), width)]
        if d == 0:
            return pltpu.make_async_copy(source, target, own_sem.at[i])
        return pltpu.make_async_remote_copy(
            src_ref=source,
            dst_ref=target,
            send_sem=send_one.at[i, d],
            recv_sem=recv_one.at[i, d],
            device_id={"gx": other},
            device_id_type=MESH,
        )

    def outer_copy(k, piece):
        row = pl.ds(pl.multiple_of(piece * SUBLANES, SUBLANES), SUBLANES)
        return pltpu.make_async_remote_copy(
            src_ref=cells_ref.at[(levels - 1, 0)[k], row, :],
            dst_ref=(under_ref, over_ref)[k].at[0, row, :],
            send_sem=outer_send.at[k, piece],
            recv_sem=outer_recv.at[k, piece],
            device_id={"grp": lax.rem(mine + (1, groups - 1)[k], groups)},
            device_id_type=MESH,
        )

    pieces = (fine_rows // SUBLANES, early_rows // SUBLANES)
    during = min(turns, pieces[0])
    ahead = pieces[0] - during

    for i in range(turns):
        for d in range(columns):
            first_copy(i, (d + 1) % columns).start()
    for piece in range(max(ahead, pieces[1])):
        if piece < ahead:
            outer_copy(0, piece).start()
        if piece < pieces[1]:
            outer_copy(1, piece).start()

    for load in loads + [late_in]:
        load.wait()
    late_out.start()
    lane_at = lax.broadcasted_iota(jnp.int32, (fine_rows, LANES), 1)
    for level in range(levels):
        row_out[0, level : level + 1, :] = edge_rows[0, level, SUBLANES - 1 : SUBLANES, :]
        row_out[1, level : level + 1, :] = edge_rows[1, level, 0:1, :]
    for k in range(2):
        packed = jnp.zeros((fine_rows, LANES), jnp.float32)
        for level in range(levels):
            column = edge_cols[k, level, :, LANES - 1 : LANES] if k == 0 else edge_cols[k, level, :, 0:1]
            packed = jnp.where(lane_at == level, column, packed)
        col_out[k] = packed
    outer = []
    for k in range(2):
        outer.append(
            pltpu.make_async_remote_copy(
                src_ref=row_out.at[k],
                dst_ref=row_in.at[k],
                send_sem=row_send.at[k],
                recv_sem=row_recv.at[k],
                device_id={"gy": (above, below)[k]},
                device_id_type=MESH,
            )
        )
        outer.append(
            pltpu.make_async_remote_copy(
                src_ref=col_out.at[k],
                dst_ref=col_in.at[k],
                send_sem=col_send.at[k],
                recv_sem=col_recv.at[k],
                device_id={"gx": lax.rem(at + (1, columns - 1)[k], columns)},
                device_id_type=MESH,
            )
        )
    for copy in outer:
        copy.start()

    def second_copy(i, b):
        group, inner, plane, row = place(at + columns * i)
        source = lines.at[i, :, pl.ds(b * width, span)]
        target = landed.at[mine, plane, pl.ds(row, SUBLANES), :]
        remote = lambda: pltpu.make_async_remote_copy(
            src_ref=source,
            dst_ref=target,
            send_sem=send_two.at[i, b],
            recv_sem=recv_two.at[mine, inner],
            device_id={"grp": group, "gx": b},
            device_id_type=MESH,
        )
        local = lambda: pltpu.make_async_copy(source, target, recv_two.at[mine, inner])
        stays = jnp.logical_and(group == mine, at == b)
        return remote, local, stays

    def one_turn(i, carry):
        for d in range(columns):
            if d == 0:
                first_copy(i, 0).wait()
            else:
                first_copy(i, d).wait_recv()
        tiles = [
            tuple(pencil[i, k, :, p * LANES : (p + 1) * LANES] for k in range(2))
            for p in range(count)
        ]
        result = transform_lines(tiles, 1.0, 1, twist_ref, table_ref, mid)
        for u, tile in enumerate(natural_tiles(result, count, turn)):
            lines[i, :, u * LANES : (u + 1) * LANES] = tile
            if u == 0:
                lines[i, :, count * LANES : (count + 1) * LANES] = tile
        for b in range(columns):
            remote, local, stays = second_copy(i, b)
            pl.when(stays)(lambda: local().start())
            pl.when(jnp.logical_not(stays))(lambda: remote().start())
        if during == turns:
            outer_copy(0, ahead + i).start()
        else:
            pl.when(i < during)(lambda: outer_copy(0, ahead + i).start())
        return carry

    lax.fori_loop(0, turns, one_turn, 0)
    for copy in outer:
        copy.wait()
    for level in range(levels):
        south_ref[level] = row_in[0, level : level + 1, :]
        north_ref[level] = row_in[1, level : level + 1, :]
        edge_ref[level] = jnp.where(
            lane_at < LANES // 2,
            col_in[1, :, level : level + 1],
            col_in[0, :, level : level + 1],
        )
    for field in range(groups):
        for inner in range(blocks):
            plane, row = inner // row_blocks, inner % row_blocks * SUBLANES
            target = landed.at[field, plane, pl.ds(row, SUBLANES), :]
            pltpu.make_async_copy(target, target, recv_two.at[field, inner]).wait()
    for field in range(groups):
        for plane in range(quarter):
            k = field * quarter + plane
            side_out[0, k : k + 1, :] = landed[field, plane, rows - 1 : rows, :]
            side_out[1, k : k + 1, :] = landed[field, plane, 0:1, :]
    sides = [
        pltpu.make_async_remote_copy(
            src_ref=side_out.at[k],
            dst_ref=side_in.at[k],
            send_sem=side_send.at[k],
            recv_sem=side_recv.at[k],
            device_id={"gy": (above, below)[k]},
            device_id_type=MESH,
        )
        for k in range(2)
    ]
    for side in sides:
        side.start()
    scale = fine_step * 0.5
    for field in range(groups - 1):
        for plane in range(quarter):
            rim_ref[field, plane, 0:rows, :] = scale * landed[field, plane]
    for side in sides:
        side.wait()
    rest = rim_ref.shape[2] - rows - 2
    for field in range(groups - 1):
        for plane in range(quarter):
            k = field * quarter + plane
            tail = jnp.concatenate(
                [
                    scale * side_in[0, k : k + 1, :],
                    scale * side_in[1, k : k + 1, :],
                    jnp.zeros((rest, span), jnp.float32),
                ],
                axis=0,
            )
            rim_ref[field, plane, rows:, :] = tail
    near, far = mean_weights()
    row_at = lax.broadcasted_iota(jnp.int32, (rows, span), 0)
    for plane in range(quarter):
        k = (groups - 1) * quarter + plane
        heat = landed[groups - 1, plane]
        before = jnp.where(row_at == 0, side_in[0, k : k + 1, :], pltpu.roll(heat, 1, 0))
        after = jnp.where(row_at == rows - 1, side_in[1, k : k + 1, :], pltpu.roll(heat, rows - 1, 0))
        heat = near * heat + far * (before + after)
        heat = near * pltpu.roll(heat, span - 1, 1) + far * (heat + pltpu.roll(heat, span - 2, 1))
        heat_ref[plane] = heat[:, :width]
    late_out.wait()
    for k in range(2):
        for piece in range(pieces[k]):
            outer_copy(k, piece).wait()
    for i in range(turns):
        for d in range(1, columns):
            first_copy(i, d).wait_send()
        for b in range(columns):
            remote, _, stays = second_copy(i, b)
            pl.when(jnp.logical_not(stays))(lambda: remote().wait_send())


def mean_weights():
    offsets = [(s + 0.5) / RATIO - 0.5 for s in range(RATIO)]
    near = sum(1.0 - abs(offset) for offset in offsets) / RATIO
    return near, (1.0 - near) / 2.0


def forward(modes, cells, early_rows, groups, columns, halves_y):
    _, planes, rows, width = modes.shape
    levels, fine_rows, fine_cols = cells.shape
    length = width * columns
    quarter = planes // groups
    blocks = quarter * (rows // SUBLANES)
    turns = groups * blocks // columns
    count = length // LANES
    span = width + LANES
    deep = -(-(rows + 2) // 16) * 16
    twist = twist_table(length, 1.0, 1)
    table = lane_table(length, 1.0, False)
    vmem = pl.BlockSpec(memory_space=pltpu.VMEM)
    dma = pltpu.SemaphoreType.DMA
    return pl.pallas_call(
        lambda *refs: forward_kernel(groups, columns, halves_y, *refs),
        name="forward_lines",
        out_shape=[
            jax.ShapeDtypeStruct((groups - 1, quarter, deep, span), jnp.float32),
            jax.ShapeDtypeStruct((quarter, rows, width), jnp.float32),
            jax.ShapeDtypeStruct((levels, fine_rows, LANES), jnp.float32),
            jax.ShapeDtypeStruct((levels, 1, fine_cols), jnp.float32),
            jax.ShapeDtypeStruct((levels, 1, fine_cols), jnp.float32),
            jax.ShapeDtypeStruct((1, fine_rows, fine_cols), jnp.float32),
            jax.ShapeDtypeStruct((1, early_rows, fine_cols), jnp.float32),
            jax.ShapeDtypeStruct((1, fine_rows - early_rows, fine_cols), jnp.float32),
        ],
        in_specs=[pl.BlockSpec(memory_space=pltpu.HBM)] * 4,
        out_specs=[vmem] * 5 + [pl.BlockSpec(memory_space=pltpu.HBM)] * 3,
        scratch_shapes=[
            pltpu.VMEM((turns, 2, SUBLANES, length), jnp.float32),
            pltpu.VMEM((2, SUBLANES * count, LANES), jnp.float32),
            pltpu.VMEM((SUBLANES * count, LANES), jnp.float32),
            pltpu.VMEM((turns, SUBLANES, length + LANES), jnp.float32),
            pltpu.VMEM((groups, quarter, rows, span), jnp.float32),
            pltpu.VMEM((2, groups * quarter, span), jnp.float32),
            pltpu.VMEM((2, groups * quarter, span), jnp.float32),
            pltpu.VMEM(twist.shape, jnp.float32),
            pltpu.VMEM(table.shape, jnp.bfloat16),
            pltpu.VMEM((2, levels, SUBLANES, fine_cols), jnp.float32),
            pltpu.VMEM((2, levels, fine_rows, LANES), jnp.float32),
            pltpu.VMEM((2, levels, fine_cols), jnp.float32),
            pltpu.VMEM((2, levels, fine_cols), jnp.float32),
            pltpu.VMEM((2, fine_rows, LANES), jnp.float32),
            pltpu.VMEM((2, fine_rows, LANES), jnp.float32),
            dma((turns, columns)),
            dma((turns, columns)),
            dma((turns,)),
            dma((turns, columns)),
            dma((groups, blocks)),
            dma((2,)),
            dma((2,)),
            dma((6,)),
            dma((2,)),
            dma((2,)),
            dma((2,)),
            dma((2,)),
            dma((2, fine_rows // SUBLANES)),
            dma((2, fine_rows // SUBLANES)),
            pltpu.VMEM((fine_rows - early_rows, fine_cols), jnp.float32),
            dma((2,)),
        ],
        compiler_params=pltpu.CompilerParams(
            collective_id=0, has_side_effects=True, vmem_limit_bytes=63 * 2**20
        ),
        cost_estimate=pl.CostEstimate(flops=10**9, bytes_accessed=10**8, transcendentals=0),
    )(modes, cells, twist, table)


def backward_kernel(
    groups,
    columns,
    rates_ref,
    cells_ref,
    modes_ref,
    damp_ref,
    twist_ref,
    table_ref,
    out_ref,
    pencil,
    mid,
    turn,
    lines,
    spectrum,
    send_one,
    recv_one,
    send_two,
    recv_two,
    send_three,
):
    mine, at = lax.axis_index("grp"), lax.axis_index("gx")
    planes, rows, width = modes_ref.shape[1:]
    quarter = planes // groups
    row_blocks = rows // SUBLANES
    blocks = quarter * row_blocks
    slots = pencil.shape[0]
    count = pencil.shape[2] // LANES
    greet(groups, columns, ())

    def where_is(block):
        return block // row_blocks, block % row_blocks * SUBLANES

    def to_worker(block):
        worker, slot = block % columns, block // columns
        plane, row = where_is(block)
        source = cells_ref.at[plane, pl.ds(row, SUBLANES), :]
        target = pencil.at[slot, :, pl.ds(pl.multiple_of(at * width, LANES), width)]
        remote = lambda: pltpu.make_async_remote_copy(
            src_ref=source,
            dst_ref=target,
            send_sem=send_one.at[block],
            recv_sem=recv_one.at[slot, at],
            device_id={"gx": worker},
            device_id_type=MESH,
        )
        local = lambda: pltpu.make_async_copy(source, target, recv_one.at[slot, at])
        return remote, local, at == worker

    for block in range(blocks):
        remote, local, stays = to_worker(block)
        pl.when(stays)(lambda: local().start())
        pl.when(jnp.logical_not(stays))(lambda: remote().start())

    def to_owner(slot, b):
        block = at + columns * slot
        plane, row = block // row_blocks, lax.rem(block, row_blocks) * SUBLANES
        row = pl.multiple_of(row, SUBLANES)
        source = lines.at[slot, :, :, pl.ds(b * width, width)]
        target = spectrum.at[:, mine * quarter + plane, pl.ds(row, SUBLANES), :]
        remote = lambda: pltpu.make_async_remote_copy(
            src_ref=source,
            dst_ref=target,
            send_sem=send_two.at[slot, b],
            recv_sem=recv_two.at[mine, block],
            device_id={"gx": b},
            device_id_type=MESH,
        )
        local = lambda: pltpu.make_async_copy(source, target, recv_two.at[mine, block])
        return remote, local, at == b

    for slot in range(slots):

        def work(slot=slot):
            for e in range(columns):
                target = pencil.at[slot, :, pl.ds(e * width, width)]
                pltpu.make_async_copy(target, target, recv_one.at[slot, e]).wait()
            tiles = [(pencil[slot, :, u * LANES : (u + 1) * LANES], None) for u in range(count)]
            result = transform_lines(tiles, -1.0, 0, twist_ref, table_ref, mid)
            for k in range(2):
                part = result[k * LANES : (k + 1) * LANES]
                for u, tile in enumerate(natural_tiles(part, count, turn)):
                    lines[slot, k, :, u * LANES : (u + 1) * LANES] = tile
            for b in range(columns):
                remote, local, stays = to_owner(slot, b)
                pl.when(stays)(lambda: local().start())
                pl.when(jnp.logical_not(stays))(lambda: remote().start())

        if blocks % columns == 0:
            work()
        else:
            pl.when(at + columns * slot < blocks)(work)

    def where_at(group, k):
        block = lax.rem(at + k, blocks)
        plane = group * quarter + block // row_blocks
        row = pl.multiple_of(lax.rem(block, row_blocks) * SUBLANES, SUBLANES)
        return block, plane, pl.ds(row, SUBLANES)

    def arrival(group, k):
        block, plane, at_rows = where_at(group, k)
        target = spectrum.at[:, plane, at_rows, :]
        return pltpu.make_async_copy(target, target, recv_two.at[group, block])

    def onward(group, k, other, slot):
        block, plane, at_rows = where_at(group, k)
        target = spectrum.at[:, plane, at_rows, :]
        return pltpu.make_async_remote_copy(
            src_ref=target,
            dst_ref=target,
            send_sem=send_three.at[k, slot],
            recv_sem=recv_two.at[group, block],
            device_id={"grp": other},
            device_id_type=MESH,
        )

    def finish(group, k):
        _, index, at_rows = where_at(group, k)
        for part in range(2):
            out_ref[part, index, at_rows, :] = (
                damp_ref[...] * modes_ref[part, index, at_rows, :]
                + rates_ref[0] * spectrum[part, index, at_rows, :]
            )

    square = groups == 4
    if square:
        pair = mine + 1 - 2 * lax.rem(mine, 2)
        across = lax.rem(mine + 2, groups)
        others = [pair, across, lax.rem(pair + 2, groups)]
        direct = 2
    else:
        others = [lax.rem(mine + d, groups) for d in range(1, groups)]
        direct = groups - 1
    sent = []
    for k in range(blocks):
        arrival(mine, k).wait()
        for slot in range(direct):
            copy = onward(mine, k, others[slot], slot)
            copy.start()
            sent.append(copy)
    for k in range(blocks):
        finish(mine, k)
    for k in range(blocks):
        for slot in range(direct):
            arrival(others[slot], k).wait()
            if square and slot == k % 2:
                copy = onward(others[slot], k, others[1 - slot], 2)
                copy.start()
                sent.append(copy)
    for slot in range(groups - 1):
        for k in range(blocks):
            if slot >= direct:
                arrival(others[slot], k).wait()
            finish(others[slot], k)
    for copy in sent:
        copy.wait_send()
    for block in range(blocks):
        remote, _, stays = to_worker(block)
        pl.when(jnp.logical_not(stays))(lambda: remote().wait_send())
    for slot in range(slots):
        for b in range(columns):
            remote, _, stays = to_owner(slot, b)
            sent = jnp.logical_not(stays)
            if blocks % columns:
                sent = jnp.logical_and(sent, at + columns * slot < blocks)
            pl.when(sent)(lambda: remote().wait_send())


def backward(gain, cells, modes, damping, groups, columns):
    _, planes, rows, width = modes.shape
    length = width * columns
    quarter = planes // groups
    blocks = quarter * (rows // SUBLANES)
    slots = -(-blocks // columns)
    count = length // LANES
    twist = twist_table(length, -1.0, 0)
    table = lane_table(length, -1.0, True)
    vmem = pl.BlockSpec(memory_space=pltpu.VMEM)
    dma = pltpu.SemaphoreType.DMA
    return pl.pallas_call(
        lambda *refs: backward_kernel(groups, columns, *refs),
        name="backward_lines",
        out_shape=jax.ShapeDtypeStruct(modes.shape, jnp.float32),
        in_specs=[pl.BlockSpec(memory_space=pltpu.SMEM)] + [vmem] * 5,
        out_specs=vmem,
        scratch_shapes=[
            pltpu.VMEM((slots, SUBLANES, length), jnp.float32),
            pltpu.VMEM((2, SUBLANES * count, LANES), jnp.float32),
            pltpu.VMEM((SUBLANES * count, LANES), jnp.float32),
            pltpu.VMEM((slots, 2, SUBLANES, length), jnp.float32),
            pltpu.VMEM(modes.shape, jnp.float32),
            dma((blocks,)),
            dma((slots, columns)),
            dma((slots, columns)),
            dma((groups, blocks)),
            dma((blocks, groups)),
        ],
        compiler_params=pltpu.CompilerParams(
            collective_id=1, has_side_effects=True, vmem_limit_bytes=32 * 2**20
        ),
        cost_estimate=pl.CostEstimate(flops=10**9, bytes_accessed=5 * 10**7, transcendentals=0),
    )(gain, cells, modes, damping, twist, table)


def rows_table(row_count, source_count):
    fine_row = np.arange(row_count * RATIO)
    parent = fine_row // RATIO
    offset = (fine_row % RATIO + 0.5) / RATIO - 0.5
    table = np.zeros((row_count * RATIO, source_count), np.float32)
    beside = np.where(
        offset > 0,
        np.where(parent == row_count - 1, row_count + 1, parent + 1),
        np.where(parent == 0, row_count, parent - 1),
    )
    table[fine_row, parent] = 1.0 - np.abs(offset)
    table[fine_row, beside] = np.abs(offset)
    return np.concatenate([table, table], axis=1).astype(jnp.bfloat16)


def lanes_table(cell_count):
    fine_cell = np.arange(cell_count * RATIO)
    parent = fine_cell // RATIO
    offset = (fine_cell % RATIO + 0.5) / RATIO - 0.5
    table = np.zeros((LANES, cell_count * RATIO), np.float32)
    table[parent + 1, fine_cell] = 1.0 - np.abs(offset)
    table[np.where(offset > 0, parent + 2, parent), fine_cell] = np.abs(offset)
    return np.concatenate([table, table], axis=0).astype(jnp.bfloat16)


def average_table(fine_count, weight):
    cell = np.arange(fine_count // RATIO)[None, :]
    table = np.where(np.arange(fine_count)[:, None] // RATIO == cell, weight, 0.0)
    return np.concatenate([table, table], axis=0).astype(jnp.bfloat16)


def split_parts(value):
    high = value.astype(jnp.bfloat16)
    return high, (value - high.astype(jnp.float32)).astype(jnp.bfloat16)


def product(left, right):
    return jnp.dot(left, right, preferred_element_type=jnp.float32)


def split_pair(value, axis):
    return jnp.concatenate(split_parts(value), axis=axis)


def block_means(total, rows_ref, lanes_ref):
    half = product(rows_ref[...], split_pair(total, 0))
    fine = LANES * RATIO
    chunks = half.shape[1] // fine
    stacked = jnp.concatenate([half[:, k * fine : (k + 1) * fine] for k in range(chunks)], axis=0)
    cells = product(split_pair(stacked, 1), lanes_ref[...])
    height = half.shape[0]
    return [cells[k * height : (k + 1) * height] for k in range(chunks)]


def fine_kernel(
    rate_ref,
    cells_hbm,
    edge_ref,
    south_ref,
    north_ref,
    under_hbm,
    over_hbm,
    rim_ref,
    heat_ref,
    ty_ref,
    tx_ref,
    ry_ref,
    rx_ref,
    out_hbm,
    coarse_ref,
    factor_ref,
    held,
    vel,
    acc,
    ready,
    in_sem,
    out_sem,
):
    plane = pl.program_id(0)
    slabs, spans, tall = held.shape[:3]
    levels, rows, cols = cells_hbm.shape
    strips, tiles = rows // SUBLANES, cols // LANES
    fields = rim_ref.shape[0]
    pieces = vel.shape[0]
    half = LANES // 2

    early = over_hbm.shape[1]

    near = min(RATIO + 1, levels)
    groups = (
        (under_hbm, 0, 1, 0),
        (cells_hbm, 0, near, 1),
        (cells_hbm, near, levels - near, near + 1),
        (over_hbm, 0, 1, slabs - 1),
    )

    def start_group(k):
        source, first, depth, slab = groups[k]

        @pl.loop(0, tiles if depth else 0)
        def _(tile):
            pltpu.make_async_copy(
                source.at[
                    pl.ds(first, depth), :, pl.ds(pl.multiple_of(tile * LANES, LANES), LANES)
                ],
                held.at[pl.ds(slab, depth), tile, pl.ds(SUBLANES, source.shape[1]), :],
                in_sem.at[k],
            ).start()

    def wait_group(k):
        source, _, depth, slab = groups[k]
        if depth:
            whole = held.at[
                pl.ds(slab, depth), pl.ds(0, tiles), pl.ds(SUBLANES, source.shape[1]), :
            ]
            pltpu.make_async_copy(whole, whole, in_sem.at[k]).wait()

    @pl.when(plane == 0)
    def _():
        start_group(0)
        start_group(1)
        empty = jnp.zeros((tiles, rows - early, LANES), jnp.float32)
        held[slabs - 1, 0:tiles, SUBLANES + early : SUBLANES + rows, :] = empty

    for part in range(RATIO):
        level = plane * RATIO + part
        held[level + 1, tiles, SUBLANES : SUBLANES + rows, :] = edge_ref[part]
        for tile in range(tiles):
            lanes = slice(tile * LANES, (tile + 1) * LANES)
            held[level + 1, tile, SUBLANES - 1 : SUBLANES, :] = south_ref[part, :, lanes]
            held[level + 1, tile, SUBLANES + rows : SUBLANES + rows + 1, :] = north_ref[part, :, lanes]

    along = jnp.concatenate(
        [product(ty_ref[...], split_pair(rim_ref[field, 0], 0)) for field in range(fields)],
        axis=0,
    )
    span = along.shape[1]
    views = [split_parts(along), split_parts(pltpu.roll(along, span - half, 1))]
    group = min(4, pieces)
    for first in range(0, pieces, group):
        windows = []
        for k in range(first, first + group):
            high, low = views[k % 2]
            lanes = slice(k // 2 * LANES, (k // 2 + 1) * LANES)
            windows.append(jnp.concatenate([high[:, lanes], low[:, lanes]], axis=1))
        refined = product(jnp.concatenate(windows, axis=0), tx_ref[...])
        for k in range(group):
            vel[first + k] = refined[k * fields * rows : (k + 1) * fields * rows]

    @pl.when(plane == 0)
    def _():
        start_group(2)
        start_group(3)
        wait_group(0)
        wait_group(1)

    top_plane = plane == pl.num_programs(0) - 1

    @pl.when(plane == (1 if levels > RATIO else 0))
    def _():
        wait_group(2)
        wait_group(3)

    side_rates = [fine_step * rate_ref[plane * RATIO + part] for part in range(RATIO)]
    own_rates = [1.0 - 6.0 * rate for rate in side_rates]
    lane_at = lax.broadcasted_iota(jnp.int32, (SUBLANES, LANES), 1)
    first_lane, last_lane = lane_at == 0, lane_at == LANES - 1
    per_turn = vel.shape[2] // LANES
    base = plane * RATIO

    def out_copy(index, strip):
        at = pl.ds(pl.multiple_of(strip * SUBLANES, SUBLANES), SUBLANES)
        block = pl.ds(index * RATIO, RATIO)
        return pltpu.make_async_copy(
            ready.at[block, at, :], out_hbm.at[block, at, :], out_sem.at[index, strip]
        )

    @pl.loop(0, strips)
    def _(s):
        start = pl.multiple_of(s * SUBLANES, SUBLANES)
        at = pl.ds(start, SUBLANES)
        middle = pl.ds(start + SUBLANES, SUBLANES)
        below, above = pl.ds(start + SUBLANES - 1, SUBLANES), pl.ds(start + SUBLANES + 1, SUBLANES)
        slabs_here = [base + part + 1 for part in range(RATIO)]
        west_turned = [pltpu.roll(held[slab, tiles, middle, :], 1, 1) for slab in slabs_here]
        centre = [held[slab, 0, middle, :] for slab in slabs_here]
        east_turned = [pltpu.roll(x, LANES - 1, 1) for x in centre]
        for tile in range(tiles):
            k, j = divmod(tile, per_turn)
            lanes = slice(tile * LANES, (tile + 1) * LANES)
            inner = slice(j * LANES, (j + 1) * LANES)
            ahead = [held[slab, tile + 1, middle, :] for slab in slabs_here]
            ahead_turned = [pltpu.roll(x, LANES - 1, 1) for x in ahead]
            here_turned = [pltpu.roll(x, 1, 1) for x in centre]
            column = (
                [held[base, tile, middle, :]] + centre + [held[base + RATIO + 1, tile, middle, :]]
            )
            flow = [
                vel[k, pl.ds(pl.multiple_of(f * rows + start, SUBLANES), SUBLANES), inner]
                for f in range(fields)
            ]
            total = None
            for part, slab in enumerate(slabs_here):
                west = jnp.where(first_lane, west_turned[part], here_turned[part])
                east = jnp.where(last_lane, ahead_turned[part], east_turned[part])
                south, north = held[slab, tile, below, :], held[slab, tile, above, :]
                lower, upper = column[part], column[part + 2]
                around = (east + west) + (north + south) + (upper + lower)
                advection = (
                    flow[0] * (east - west)
                    + flow[1] * (north - south)
                    + flow[2] * (upper - lower)
                )
                updated = own_rates[part] * centre[part] + side_rates[part] * around - advection
                ready[base + part, at, lanes] = updated
                total = updated if total is None else total + updated
            acc[at, lanes] = total
            west_turned, centre, east_turned = here_turned, ahead, ahead_turned
        out_copy(plane, s).start()

    for k, cells in enumerate(block_means(acc[...], ry_ref, rx_ref)):
        lanes = slice(k * LANES, (k + 1) * LANES)
        coarse_ref[0, :, lanes] = heat_ref[0, :, lanes] - cells

    @pl.when(top_plane)
    def _():
        wide = vel.shape[2]
        for k in range(pieces):
            factor_ref[:, k * wide : (k + 1) * wide] = (
                side_rates[RATIO - 1] - vel[k, (fields - 1) * rows + early : fields * rows, :]
            )

    @pl.when(top_plane)
    def _():
        for index in range(levels // RATIO):
            for s in range(strips):
                out_copy(index, s).wait()


def fine_update(rimmed, heat, edge, south, north, under, over, salinity, diffusivity):
    levels, rows, cols = salinity.shape
    fields, quarter = rimmed.shape[:2]
    row_count, width = rows // RATIO, cols // RATIO
    cell_count = LANES // 2
    late_rows = rows - over.shape[1]
    ty = rows_table(row_count, rimmed.shape[2])
    tx = lanes_table(cell_count)
    ry = average_table(rows, 1.0 / RATIO).T
    rx = average_table(LANES * RATIO, 1.0 / RATIO / RATIO)
    pieces = width // cell_count

    def fixed(array):
        return pl.BlockSpec(array.shape, lambda i: (0,) * array.ndim)

    hbm = pl.BlockSpec(memory_space=pltpu.HBM)
    return pl.pallas_call(
        fine_kernel,
        name="fine_levels",
        grid=(quarter,),
        in_specs=[
            pl.BlockSpec(memory_space=pltpu.SMEM),
            hbm,
            pl.BlockSpec((RATIO, rows, LANES), lambda i: (i, 0, 0)),
            pl.BlockSpec((RATIO, 1, cols), lambda i: (i, 0, 0)),
            pl.BlockSpec((RATIO, 1, cols), lambda i: (i, 0, 0)),
            hbm,
            hbm,
            pl.BlockSpec((fields, 1) + rimmed.shape[2:], lambda i: (0, i, 0, 0)),
            pl.BlockSpec((1, row_count, width), lambda i: (i, 0, 0)),
            fixed(ty),
            fixed(tx),
            fixed(ry),
            fixed(rx),
        ],
        out_specs=[
            hbm,
            pl.BlockSpec((1, row_count, width), lambda i: (i, 0, 0)),
            pl.BlockSpec((late_rows, cols), lambda i: (0, 0)),
        ],
        out_shape=[
            jax.ShapeDtypeStruct(salinity.shape, jnp.float32),
            jax.ShapeDtypeStruct((quarter, row_count, width), jnp.float32),
            jax.ShapeDtypeStruct((late_rows, cols), jnp.float32),
        ],
        scratch_shapes=[
            pltpu.VMEM((levels + 2, cols // LANES + 1, rows + 2 * SUBLANES, LANES), jnp.float32),
            pltpu.VMEM((pieces, fields * rows, cell_count * RATIO), jnp.float32),
            pltpu.VMEM((rows, cols), jnp.float32),
            pltpu.VMEM((levels, rows, cols), jnp.float32),
            pltpu.SemaphoreType.DMA((4,)),
            pltpu.SemaphoreType.DMA((quarter, rows // SUBLANES)),
        ],
        compiler_params=pltpu.CompilerParams(
            dimension_semantics=("arbitrary",), vmem_limit_bytes=59 * 2**20
        ),
        cost_estimate=pl.CostEstimate(flops=10**9, bytes_accessed=4 * 10**7, transcendentals=0),
    )(diffusivity, salinity, edge, south, north, under, over, rimmed, heat, ty, tx, ry, rx)


def outer_kernel(
    level_hbm,
    factor_hbm,
    over_hbm,
    cells_hbm,
    ry_hbm,
    rx_hbm,
    out_hbm,
    coarse_ref,
    held,
    factor_ref,
    over_ref,
    ry_ref,
    rx_ref,
    in_sem,
    out_sem,
):
    levels, rows = out_hbm.shape[:2]
    late = held.shape[0]
    plane = coarse_ref.shape[0] - 1
    place = out_hbm.at[levels - 1, pl.ds(rows - late, late), :]
    pairs = (
        (factor_hbm, factor_ref),
        (over_hbm.at[0], over_ref),
        (ry_hbm, ry_ref),
        (rx_hbm, rx_ref),
        (place, held),
        (cells_hbm, coarse_ref),
    )
    loads = [
        pltpu.make_async_copy(source, target, in_sem.at[k])
        for k, (source, target) in enumerate(pairs)
    ]
    for load in loads:
        load.start()
    for load in loads:
        load.wait()
    added = factor_ref[...] * over_ref[...]
    held[...] = held[...] + added
    store = pltpu.make_async_copy(held, place, out_sem.at[0])
    store.start()
    for k, cells in enumerate(block_means(added, ry_ref, rx_ref)):
        lanes = slice(k * LANES, (k + 1) * LANES)
        coarse_ref[plane, :, lanes] = coarse_ref[plane, :, lanes] - cells
    store.wait()


def outer_update(levels_next, factor, over, cells):
    rows = levels_next.shape[1]
    late = factor.shape[0]
    ry = average_table(rows, 1.0 / RATIO)[rows - late : rows].T
    ry = np.concatenate([ry, ry], axis=1)
    rx = average_table(LANES * RATIO, 1.0 / RATIO / RATIO)
    hbm = pl.BlockSpec(memory_space=pltpu.HBM)
    return pl.pallas_call(
        outer_kernel,
        name="outer_levels",
        in_specs=[hbm] * 6,
        out_specs=[hbm, pl.BlockSpec(memory_space=pltpu.VMEM)],
        out_shape=[
            jax.ShapeDtypeStruct(levels_next.shape, jnp.float32),
            jax.ShapeDtypeStruct(cells.shape, jnp.float32),
        ],
        scratch_shapes=[
            pltpu.VMEM(factor.shape, jnp.float32),
            pltpu.VMEM(factor.shape, jnp.float32),
            pltpu.VMEM(factor.shape, jnp.float32),
            pltpu.VMEM(ry.shape, jnp.bfloat16),
            pltpu.VMEM(rx.shape, jnp.bfloat16),
            pltpu.SemaphoreType.DMA((6,)),
            pltpu.SemaphoreType.DMA((1,)),
        ],
        input_output_aliases={0: 0},
        compiler_params=pltpu.CompilerParams(vmem_limit_bytes=59 * 2**20),
        cost_estimate=pl.CostEstimate(flops=10**8, bytes_accessed=4 * 10**6, transcendentals=0),
    )(levels_next, factor, over, cells, ry, rx)


def from_above(layer, axis):
    count = lax.axis_size(axis)
    return lax.ppermute(layer, axis, [((i + 1) % count, i) for i in range(count)])


def per_device(coarse_modes, salinity, viscosity, forcing_gain, diffusivity):
    width = coarse_modes.shape[4]
    groups, columns = lax.axis_size("grp"), lax.axis_size("gx")
    early_rows = salinity.shape[1] - LATE_PIECES * SUBLANES
    rimmed, heat, edge, south, north, under, over, low = forward(
        coarse_modes[0], salinity, early_rows, groups, columns, lax.axis_size("gy")
    )
    over_late = from_above(low, "grp")
    partial_next, partial_cells, factor = fine_update(
        rimmed, heat, edge, south, north, under, over, salinity, diffusivity
    )
    salinity_next, restricted = outer_update(partial_next, factor, over_late, partial_cells)
    total_modes = width * columns
    mode_index = lax.axis_index("gx") * width + lax.broadcasted_iota(jnp.int32, (1, width), 1)
    wavenumber = jnp.where(mode_index < total_modes // 2, mode_index, mode_index - total_modes)
    scaled_wave = 2.0 * math.pi / total_modes * wavenumber.astype(jnp.float32)
    damping = jnp.exp(-viscosity[0] * scaled_wave * scaled_wave)
    coarse_next = backward(forcing_gain, restricted, coarse_modes[0], damping, groups, columns)
    return (salinity_next, coarse_next[None])


def solution(mesh):
    return jax.shard_map(
        per_device,
        mesh=mesh,
        in_specs=(
            P("grp", None, None, "gy", "gx"),
            P("grp", "gy", "gx"),
            P("grp"),
            P("grp"),
            P("grp"),
        ),
        out_specs=(P("grp", "gy", "gx"), P("grp", None, None, "gy", "gx")),
        check_vma=False,
    )
```

```python
import math

import jax
import jax.numpy as jnp
import numpy as np
from jax import lax
from jax.experimental import pallas as pl
from jax.experimental.pallas import tpu as pltpu
from jax.sharding import PartitionSpec as P

RATIO = 4
LATE_PIECES = 5


fine_step = 0.1


LANES = 128
SUBLANES = 8
MESH = pl.DeviceIdType.MESH


def turn_table(rows, cols, period, orient, shift):
    product = np.outer(np.arange(rows) - shift, np.arange(cols)) % period
    angle = 2.0 * np.pi / period * product
    return np.cos(angle), orient * np.sin(angle)


def twist_table(length, orient, shift):
    cosine, sine = turn_table(length // LANES, LANES, length, orient, shift)
    return (np.stack([cosine, sine]) * length ** (-0.25)).astype(np.float32)


def lane_table(length, orient, want_imag):
    tiles = length // LANES
    groups = LANES // tiles
    order = (np.arange(tiles)[None, :] * groups + np.arange(groups)[:, None]).reshape(-1)
    cosine, sine = turn_table(LANES, LANES, LANES, orient, 0)
    cosine, sine = cosine[order], sine[order]
    table = np.concatenate([cosine, -sine], axis=1)
    if want_imag:
        table = np.concatenate([table, np.concatenate([sine, cosine], axis=1)], axis=0)
    table = (table * length ** (-0.25)).astype(np.float32)
    high = table.astype(jnp.bfloat16)
    low = (table - high.astype(np.float32)).astype(jnp.bfloat16)
    return np.concatenate([high, low, high], axis=1)


def butterflies(parts, orient):
    count = len(parts)
    if count == 1:
        return parts
    even = butterflies(parts[0::2], orient)
    odd = butterflies(parts[1::2], orient)
    sums, differences = [], []
    for k in range(count // 2):
        real, imag = odd[k]
        if k == 0:
            turned = (real, imag)
        elif 4 * k == count:
            turned = (None if imag is None else -orient * imag, orient * real)
        else:
            angle = orient * 2.0 * math.pi * k / count
            cosine, sine = math.cos(angle), math.sin(angle)
            if imag is None:
                turned = (cosine * real, sine * real)
            else:
                turned = (cosine * real - sine * imag, sine * real + cosine * imag)
        first = even[k]
        sums.append((plus(first[0], turned[0]), plus(first[1], turned[1])))
        differences.append((minus(first[0], turned[0]), minus(first[1], turned[1])))
    return sums + differences


def plus(left, right):
    if left is None:
        return right
    return left if right is None else left + right


def minus(left, right):
    if right is None:
        return left
    return -right if left is None else left - right


def split_stack(value):
    high, low = split_parts(value)
    return jnp.concatenate([high, high, low], axis=1)


def transform_lines(tiles, orient, shift, twist_ref, table_ref, mid_ref):
    count = len(tiles)
    bins = butterflies(tiles, orient)
    for r in range(count):
        real, imag = bins[(r - shift) % count]
        cosine, sine = twist_ref[0, r : r + 1, :], twist_ref[1, r : r + 1, :]
        at = slice(r * SUBLANES, (r + 1) * SUBLANES)
        if imag is None:
            mid_ref[0, at, :], mid_ref[1, at, :] = real * cosine, real * sine
        else:
            mid_ref[0, at, :] = real * cosine - imag * sine
            mid_ref[1, at, :] = real * sine + imag * cosine
    parts = [
        jnp.concatenate(
            [mid_ref[k, pl.ds(row, count, stride=SUBLANES), :] for row in range(SUBLANES)], axis=0
        )
        for k in range(2)
    ]
    stacked = split_stack(jnp.concatenate(parts, axis=1))
    return lax.dot_general(
        table_ref[...], stacked, (((1,), (1,)), ((), ())), preferred_element_type=jnp.float32
    )


def natural_tiles(result, count, turn_ref):
    groups = LANES // count
    group_at = lax.broadcasted_iota(jnp.int32, (count, LANES), 1) // count
    for tile in range(SUBLANES // groups):
        lanes = slice(tile * LANES, (tile + 1) * LANES)
        pieces = [result[k * count : (k + 1) * count, lanes] for k in range(groups)]
        for row in range(groups):
            line = None
            for k in range(groups):
                shift = count * (k - row) % LANES
                moved = pieces[k] if shift == 0 else pltpu.roll(pieces[k], shift, 1)
                line = moved if line is None else jnp.where(group_at == k, moved, line)
            start = (tile * groups + row) * count
            turn_ref[start : start + count, :] = line
    return [turn_ref[pl.ds(u, SUBLANES, stride=count), :] for u in range(count)]


def greet(groups, columns, neighbours):
    barrier = pltpu.get_barrier_semaphore()
    mine, at = lax.axis_index("grp"), lax.axis_index("gx")
    total = 0
    for d in range(groups):
        for e in range(columns):
            if d == 0 and e == 0:
                continue
            pl.semaphore_signal(
                barrier,
                inc=1,
                device_id={"grp": lax.rem(mine + d, groups), "gx": lax.rem(at + e, columns)},
                device_id_type=MESH,
            )
            total += 1
    for neighbour in neighbours:
        pl.semaphore_signal(barrier, inc=1, device_id={"gy": neighbour}, device_id_type=MESH)
        total += 1
    pl.semaphore_wait(barrier, total)


def forward_kernel(
    groups,
    columns,
    halves_y,
    modes_ref,
    cells_ref,
    twist_hbm,
    table_hbm,
    rim_ref,
    heat_ref,
    edge_ref,
    south_ref,
    north_ref,
    under_ref,
    over_ref,
    low_ref,
    pencil,
    mid,
    turn,
    lines,
    landed,
    side_out,
    side_in,
    twist_ref,
    table_ref,
    edge_rows,
    edge_cols,
    row_out,
    row_in,
    col_out,
    col_in,
    send_one,
    recv_one,
    own_sem,
    send_two,
    recv_two,
    side_send,
    side_recv,
    load_sem,
    row_send,
    row_recv,
    col_send,
    col_recv,
    outer_send,
    outer_recv,
    late,
    late_sem,
):
    mine, at, half = lax.axis_index("grp"), lax.axis_index("gx"), lax.axis_index("gy")
    above, below = lax.rem(half + 1, halves_y), lax.rem(half + halves_y - 1, halves_y)
    planes, rows, width = modes_ref.shape[1:]
    quarter = planes // groups
    row_blocks = rows // SUBLANES
    blocks = quarter * row_blocks
    turns = pencil.shape[0]
    count = pencil.shape[3] // LANES
    span = width + LANES
    levels, fine_rows, fine_cols = cells_ref.shape
    loads = [
        pltpu.make_async_copy(source, target, load_sem.at[k])
        for k, (source, target) in enumerate(
            (
                (cells_ref.at[:, pl.ds(fine_rows - SUBLANES, SUBLANES), :], edge_rows.at[0]),
                (cells_ref.at[:, pl.ds(0, SUBLANES), :], edge_rows.at[1]),
                (cells_ref.at[:, :, pl.ds(fine_cols - LANES, LANES)], edge_cols.at[0]),
                (cells_ref.at[:, :, pl.ds(0, LANES)], edge_cols.at[1]),
                (twist_hbm, twist_ref),
                (table_hbm, table_ref),
            )
        )
    ]
    early_rows = over_ref.shape[1]
    late_rows = pl.ds(early_rows, fine_rows - early_rows)
    late_in = pltpu.make_async_copy(cells_ref.at[0, late_rows, :], late, late_sem.at[0])
    late_out = pltpu.make_async_copy(late, low_ref.at[0], late_sem.at[1])
    for load in loads + [late_in]:
        load.start()
    greet(groups, columns, (above, below))

    def place(block):
        group, inner = block // blocks, lax.rem(block, blocks)
        plane = inner // row_blocks
        row = pl.multiple_of(lax.rem(inner, row_blocks) * SUBLANES, SUBLANES)
        return group, inner, plane, row

    def first_copy(i, d):
        other = lax.rem(at + d, columns)
        group, _, plane, row = place(other + columns * i)
        source = modes_ref.at[:, group * quarter + plane, pl.ds(row, SUBLANES), :]
        target = pencil.at[i, :, :, pl.ds(pl.multiple_of(at * width, LANES), width)]
        if d == 0:
            return pltpu.make_async_copy(source, target, own_sem.at[i])
        return pltpu.make_async_remote_copy(
            src_ref=source,
            dst_ref=target,
            send_sem=send_one.at[i, d],
            recv_sem=recv_one.at[i, d],
            device_id={"gx": other},
            device_id_type=MESH,
        )

    def outer_copy(k, piece):
        row = pl.ds(pl.multiple_of(piece * SUBLANES, SUBLANES), SUBLANES)
        return pltpu.make_async_remote_copy(
            src_ref=cells_ref.at[(levels - 1, 0)[k], row, :],
            dst_ref=(under_ref, over_ref)[k].at[0, row, :],
            send_sem=outer_send.at[k, piece],
            recv_sem=outer_recv.at[k, piece],
            device_id={"grp": lax.rem(mine + (1, groups - 1)[k], groups)},
            device_id_type=MESH,
        )

    pieces = (fine_rows // SUBLANES, early_rows // SUBLANES)
    during = min(turns, pieces[0])
    ahead = pieces[0] - during

    for i in range(turns):
        for d in range(columns):
            first_copy(i, (d + 1) % columns).start()
    for piece in range(max(ahead, pieces[1])):
        if piece < ahead:
            outer_copy(0, piece).start()
        if piece < pieces[1]:
            outer_copy(1, piece).start()

    for load in loads + [late_in]:
        load.wait()
    late_out.start()
    lane_at = lax.broadcasted_iota(jnp.int32, (fine_rows, LANES), 1)
    for level in range(levels):
        row_out[0, level : level + 1, :] = edge_rows[0, level, SUBLANES - 1 : SUBLANES, :]
        row_out[1, level : level + 1, :] = edge_rows[1, level, 0:1, :]
    for k in range(2):
        packed = jnp.zeros((fine_rows, LANES), jnp.float32)
        for level in range(levels):
            column = edge_cols[k, level, :, LANES - 1 : LANES] if k == 0 else edge_cols[k, level, :, 0:1]
            packed = jnp.where(lane_at == level, column, packed)
        col_out[k] = packed
    outer = []
    for k in range(2):
        outer.append(
            pltpu.make_async_remote_copy(
                src_ref=row_out.at[k],
                dst_ref=row_in.at[k],
                send_sem=row_send.at[k],
                recv_sem=row_recv.at[k],
                device_id={"gy": (above, below)[k]},
                device_id_type=MESH,
            )
        )
        outer.append(
            pltpu.make_async_remote_copy(
                src_ref=col_out.at[k],
                dst_ref=col_in.at[k],
                send_sem=col_send.at[k],
                recv_sem=col_recv.at[k],
                device_id={"gx": lax.rem(at + (1, columns - 1)[k], columns)},
                device_id_type=MESH,
            )
        )
    for copy in outer:
        copy.start()

    def second_copy(i, b):
        group, inner, plane, row = place(at + columns * i)
        source = lines.at[i, :, pl.ds(b * width, span)]
        target = landed.at[mine, plane, pl.ds(row, SUBLANES), :]
        remote = lambda: pltpu.make_async_remote_copy(
            src_ref=source,
            dst_ref=target,
            send_sem=send_two.at[i, b],
            recv_sem=recv_two.at[mine, inner],
            device_id={"grp": group, "gx": b},
            device_id_type=MESH,
        )
        local = lambda: pltpu.make_async_copy(source, target, recv_two.at[mine, inner])
        stays = jnp.logical_and(group == mine, at == b)
        return remote, local, stays

    def one_turn(i, carry):
        for d in range(columns):
            if d == 0:
                first_copy(i, 0).wait()
            else:
                first_copy(i, d).wait_recv()
        tiles = [
            tuple(pencil[i, k, :, p * LANES : (p + 1) * LANES] for k in range(2))
            for p in range(count)
        ]
        result = transform_lines(tiles, 1.0, 1, twist_ref, table_ref, mid)
        for u, tile in enumerate(natural_tiles(result, count, turn)):
            lines[i, :, u * LANES : (u + 1) * LANES] = tile
            if u == 0:
                lines[i, :, count * LANES : (count + 1) * LANES] = tile
        for b in range(columns):
            remote, local, stays = second_copy(i, b)
            pl.when(stays)(lambda: local().start())
            pl.when(jnp.logical_not(stays))(lambda: remote().start())
        if during == turns:
            outer_copy(0, ahead + i).start()
        else:
            pl.when(i < during)(lambda: outer_copy(0, ahead + i).start())
        return carry

    lax.fori_loop(0, turns, one_turn, 0)
    for copy in outer:
        copy.wait()
    for level in range(levels):
        south_ref[level] = row_in[0, level : level + 1, :]
        north_ref[level] = row_in[1, level : level + 1, :]
        edge_ref[level] = jnp.where(
            lane_at < LANES // 2,
            col_in[1, :, level : level + 1],
            col_in[0, :, level : level + 1],
        )
    for field in range(groups):
        for inner in range(blocks):
            plane, row = inner // row_blocks, inner % row_blocks * SUBLANES
            target = landed.at[field, plane, pl.ds(row, SUBLANES), :]
            pltpu.make_async_copy(target, target, recv_two.at[field, inner]).wait()
    for field in range(groups):
        for plane in range(quarter):
            k = field * quarter + plane
            side_out[0, k : k + 1, :] = landed[field, plane, rows - 1 : rows, :]
            side_out[1, k : k + 1, :] = landed[field, plane, 0:1, :]
    sides = [
        pltpu.make_async_remote_copy(
            src_ref=side_out.at[k],
            dst_ref=side_in.at[k],
            send_sem=side_send.at[k],
            recv_sem=side_recv.at[k],
            device_id={"gy": (above, below)[k]},
            device_id_type=MESH,
        )
        for k in range(2)
    ]
    for side in sides:
        side.start()
    scale = fine_step * 0.5
    for field in range(groups - 1):
        for plane in range(quarter):
            rim_ref[field, plane, 0:rows, :] = scale * landed[field, plane]
    for side in sides:
        side.wait()
    rest = rim_ref.shape[2] - rows - 2
    for field in range(groups - 1):
        for plane in range(quarter):
            k = field * quarter + plane
            tail = jnp.concatenate(
                [
                    scale * side_in[0, k : k + 1, :],
                    scale * side_in[1, k : k + 1, :],
                    jnp.zeros((rest, span), jnp.float32),
                ],
                axis=0,
            )
            rim_ref[field, plane, rows:, :] = tail
    near, far = mean_weights()
    row_at = lax.broadcasted_iota(jnp.int32, (rows, span), 0)
    for plane in range(quarter):
        k = (groups - 1) * quarter + plane
        heat = landed[groups - 1, plane]
        before = jnp.where(row_at == 0, side_in[0, k : k + 1, :], pltpu.roll(heat, 1, 0))
        after = jnp.where(row_at == rows - 1, side_in[1, k : k + 1, :], pltpu.roll(heat, rows - 1, 0))
        heat = near * heat + far * (before + after)
        heat = near * pltpu.roll(heat, span - 1, 1) + far * (heat + pltpu.roll(heat, span - 2, 1))
        heat_ref[plane] = heat[:, :width]
    late_out.wait()
    for k in range(2):
        for piece in range(pieces[k]):
            outer_copy(k, piece).wait()
    for i in range(turns):
        for d in range(1, columns):
            first_copy(i, d).wait_send()
        for b in range(columns):
            remote, _, stays = second_copy(i, b)
            pl.when(jnp.logical_not(stays))(lambda: remote().wait_send())


def mean_weights():
    offsets = [(s + 0.5) / RATIO - 0.5 for s in range(RATIO)]
    near = sum(1.0 - abs(offset) for offset in offsets) / RATIO
    return near, (1.0 - near) / 2.0


def forward(modes, cells, early_rows, groups, columns, halves_y):
    _, planes, rows, width = modes.shape
    levels, fine_rows, fine_cols = cells.shape
    length = width * columns
    quarter = planes // groups
    blocks = quarter * (rows // SUBLANES)
    turns = groups * blocks // columns
    count = length // LANES
    span = width + LANES
    deep = -(-(rows + 2) // 16) * 16
    twist = twist_table(length, 1.0, 1)
    table = lane_table(length, 1.0, False)
    vmem = pl.BlockSpec(memory_space=pltpu.VMEM)
    dma = pltpu.SemaphoreType.DMA
    return pl.pallas_call(
        lambda *refs: forward_kernel(groups, columns, halves_y, *refs),
        name="forward_lines",
        out_shape=[
            jax.ShapeDtypeStruct((groups - 1, quarter, deep, span), jnp.float32),
            jax.ShapeDtypeStruct((quarter, rows, width), jnp.float32),
            jax.ShapeDtypeStruct((levels, fine_rows, LANES), jnp.float32),
            jax.ShapeDtypeStruct((levels, 1, fine_cols), jnp.float32),
            jax.ShapeDtypeStruct((levels, 1, fine_cols), jnp.float32),
            jax.ShapeDtypeStruct((1, fine_rows, fine_cols), jnp.float32),
            jax.ShapeDtypeStruct((1, early_rows, fine_cols), jnp.float32),
            jax.ShapeDtypeStruct((1, fine_rows - early_rows, fine_cols), jnp.float32),
        ],
        in_specs=[pl.BlockSpec(memory_space=pltpu.HBM)] * 4,
        out_specs=[vmem] * 5 + [pl.BlockSpec(memory_space=pltpu.HBM)] * 3,
        scratch_shapes=[
            pltpu.VMEM((turns, 2, SUBLANES, length), jnp.float32),
            pltpu.VMEM((2, SUBLANES * count, LANES), jnp.float32),
            pltpu.VMEM((SUBLANES * count, LANES), jnp.float32),
            pltpu.VMEM((turns, SUBLANES, length + LANES), jnp.float32),
            pltpu.VMEM((groups, quarter, rows, span), jnp.float32),
            pltpu.VMEM((2, groups * quarter, span), jnp.float32),
            pltpu.VMEM((2, groups * quarter, span), jnp.float32),
            pltpu.VMEM(twist.shape, jnp.float32),
            pltpu.VMEM(table.shape, jnp.bfloat16),
            pltpu.VMEM((2, levels, SUBLANES, fine_cols), jnp.float32),
            pltpu.VMEM((2, levels, fine_rows, LANES), jnp.float32),
            pltpu.VMEM((2, levels, fine_cols), jnp.float32),
            pltpu.VMEM((2, levels, fine_cols), jnp.float32),
            pltpu.VMEM((2, fine_rows, LANES), jnp.float32),
            pltpu.VMEM((2, fine_rows, LANES), jnp.float32),
            dma((turns, columns)),
            dma((turns, columns)),
            dma((turns,)),
            dma((turns, columns)),
            dma((groups, blocks)),
            dma((2,)),
            dma((2,)),
            dma((6,)),
            dma((2,)),
            dma((2,)),
            dma((2,)),
            dma((2,)),
            dma((2, fine_rows // SUBLANES)),
            dma((2, fine_rows // SUBLANES)),
            pltpu.VMEM((fine_rows - early_rows, fine_cols), jnp.float32),
            dma((2,)),
        ],
        compiler_params=pltpu.CompilerParams(
            collective_id=0, has_side_effects=True, vmem_limit_bytes=63 * 2**20
        ),
        cost_estimate=pl.CostEstimate(flops=10**9, bytes_accessed=10**8, transcendentals=0),
    )(modes, cells, twist, table)


def backward_kernel(
    groups,
    columns,
    rates_ref,
    cells_ref,
    modes_ref,
    damp_ref,
    twist_ref,
    table_ref,
    out_ref,
    pencil,
    mid,
    turn,
    lines,
    spectrum,
    send_one,
    recv_one,
    send_two,
    recv_two,
    send_three,
):
    mine, at = lax.axis_index("grp"), lax.axis_index("gx")
    planes, rows, width = modes_ref.shape[1:]
    quarter = planes // groups
    row_blocks = rows // SUBLANES
    blocks = quarter * row_blocks
    slots = pencil.shape[0]
    count = pencil.shape[2] // LANES
    greet(groups, columns, ())

    def where_is(block):
        return block // row_blocks, block % row_blocks * SUBLANES

    def to_worker(block):
        worker, slot = block % columns, block // columns
        plane, row = where_is(block)
        source = cells_ref.at[plane, pl.ds(row, SUBLANES), :]
        target = pencil.at[slot, :, pl.ds(pl.multiple_of(at * width, LANES), width)]
        remote = lambda: pltpu.make_async_remote_copy(
            src_ref=source,
            dst_ref=target,
            send_sem=send_one.at[block],
            recv_sem=recv_one.at[slot, at],
            device_id={"gx": worker},
            device_id_type=MESH,
        )
        local = lambda: pltpu.make_async_copy(source, target, recv_one.at[slot, at])
        return remote, local, at == worker

    for block in range(blocks):
        remote, local, stays = to_worker(block)
        pl.when(stays)(lambda: local().start())
        pl.when(jnp.logical_not(stays))(lambda: remote().start())

    def to_owner(slot, b):
        block = at + columns * slot
        plane, row = block // row_blocks, lax.rem(block, row_blocks) * SUBLANES
        row = pl.multiple_of(row, SUBLANES)
        source = lines.at[slot, :, :, pl.ds(b * width, width)]
        target = spectrum.at[:, mine * quarter + plane, pl.ds(row, SUBLANES), :]
        remote = lambda: pltpu.make_async_remote_copy(
            src_ref=source,
            dst_ref=target,
            send_sem=send_two.at[slot, b],
            recv_sem=recv_two.at[mine, block],
            device_id={"gx": b},
            device_id_type=MESH,
        )
        local = lambda: pltpu.make_async_copy(source, target, recv_two.at[mine, block])
        return remote, local, at == b

    for slot in range(slots):

        def work(slot=slot):
            for e in range(columns):
                target = pencil.at[slot, :, pl.ds(e * width, width)]
                pltpu.make_async_copy(target, target, recv_one.at[slot, e]).wait()
            tiles = [(pencil[slot, :, u * LANES : (u + 1) * LANES], None) for u in range(count)]
            result = transform_lines(tiles, -1.0, 0, twist_ref, table_ref, mid)
            for k in range(2):
                part = result[k * LANES : (k + 1) * LANES]
                for u, tile in enumerate(natural_tiles(part, count, turn)):
                    lines[slot, k, :, u * LANES : (u + 1) * LANES] = tile
            for b in range(columns):
                remote, local, stays = to_owner(slot, b)
                pl.when(stays)(lambda: local().start())
                pl.when(jnp.logical_not(stays))(lambda: remote().start())

        if blocks % columns == 0:
            work()
        else:
            pl.when(at + columns * slot < blocks)(work)

    def where_at(group, k):
        block = lax.rem(at + k, blocks)
        plane = group * quarter + block // row_blocks
        row = pl.multiple_of(lax.rem(block, row_blocks) * SUBLANES, SUBLANES)
        return block, plane, pl.ds(row, SUBLANES)

    def arrival(group, k):
        block, plane, at_rows = where_at(group, k)
        target = spectrum.at[:, plane, at_rows, :]
        return pltpu.make_async_copy(target, target, recv_two.at[group, block])

    def onward(group, k, other, slot):
        block, plane, at_rows = where_at(group, k)
        target = spectrum.at[:, plane, at_rows, :]
        return pltpu.make_async_remote_copy(
            src_ref=target,
            dst_ref=target,
            send_sem=send_three.at[k, slot],
            recv_sem=recv_two.at[group, block],
            device_id={"grp": other},
            device_id_type=MESH,
        )

    def finish(group, k):
        _, index, at_rows = where_at(group, k)
        for part in range(2):
            out_ref[part, index, at_rows, :] = (
                damp_ref[...] * modes_ref[part, index, at_rows, :]
                + rates_ref[0] * spectrum[part, index, at_rows, :]
            )

    square = groups == 4
    if square:
        pair = mine + 1 - 2 * lax.rem(mine, 2)
        across = lax.rem(mine + 2, groups)
        others = [pair, across, lax.rem(pair + 2, groups)]
        direct = 2
    else:
        others = [lax.rem(mine + d, groups) for d in range(1, groups)]
        direct = groups - 1
    sent = []
    for k in range(blocks):
        arrival(mine, k).wait()
        for slot in range(direct):
            copy = onward(mine, k, others[slot], slot)
            copy.start()
            sent.append(copy)
    for k in range(blocks):
        finish(mine, k)
    for k in range(blocks):
        for slot in range(direct):
            arrival(others[slot], k).wait()
            if square and slot == k % 2:
                copy = onward(others[slot], k, others[1 - slot], 2)
                copy.start()
                sent.append(copy)
    for slot in range(groups - 1):
        for k in range(blocks):
            if slot >= direct:
                arrival(others[slot], k).wait()
            finish(others[slot], k)
    for copy in sent:
        copy.wait_send()
    for block in range(blocks):
        remote, _, stays = to_worker(block)
        pl.when(jnp.logical_not(stays))(lambda: remote().wait_send())
    for slot in range(slots):
        for b in range(columns):
            remote, _, stays = to_owner(slot, b)
            sent = jnp.logical_not(stays)
            if blocks % columns:
                sent = jnp.logical_and(sent, at + columns * slot < blocks)
            pl.when(sent)(lambda: remote().wait_send())


def backward(gain, cells, modes, damping, groups, columns):
    _, planes, rows, width = modes.shape
    length = width * columns
    quarter = planes // groups
    blocks = quarter * (rows // SUBLANES)
    slots = -(-blocks // columns)
    count = length // LANES
    twist = twist_table(length, -1.0, 0)
    table = lane_table(length, -1.0, True)
    vmem = pl.BlockSpec(memory_space=pltpu.VMEM)
    dma = pltpu.SemaphoreType.DMA
    return pl.pallas_call(
        lambda *refs: backward_kernel(groups, columns, *refs),
        name="backward_lines",
        out_shape=jax.ShapeDtypeStruct(modes.shape, jnp.float32),
        in_specs=[pl.BlockSpec(memory_space=pltpu.SMEM)] + [vmem] * 5,
        out_specs=vmem,
        scratch_shapes=[
            pltpu.VMEM((slots, SUBLANES, length), jnp.float32),
            pltpu.VMEM((2, SUBLANES * count, LANES), jnp.float32),
            pltpu.VMEM((SUBLANES * count, LANES), jnp.float32),
            pltpu.VMEM((slots, 2, SUBLANES, length), jnp.float32),
            pltpu.VMEM(modes.shape, jnp.float32),
            dma((blocks,)),
            dma((slots, columns)),
            dma((slots, columns)),
            dma((groups, blocks)),
            dma((blocks, groups)),
        ],
        compiler_params=pltpu.CompilerParams(
            collective_id=1, has_side_effects=True, vmem_limit_bytes=32 * 2**20
        ),
        cost_estimate=pl.CostEstimate(flops=10**9, bytes_accessed=5 * 10**7, transcendentals=0),
    )(gain, cells, modes, damping, twist, table)


def rows_table(row_count, source_count):
    fine_row = np.arange(row_count * RATIO)
    parent = fine_row // RATIO
    offset = (fine_row % RATIO + 0.5) / RATIO - 0.5
    table = np.zeros((row_count * RATIO, source_count), np.float32)
    beside = np.where(
        offset > 0,
        np.where(parent == row_count - 1, row_count + 1, parent + 1),
        np.where(parent == 0, row_count, parent - 1),
    )
    table[fine_row, parent] = 1.0 - np.abs(offset)
    table[fine_row, beside] = np.abs(offset)
    return np.concatenate([table, table], axis=1).astype(jnp.bfloat16)


def lanes_table(cell_count):
    fine_cell = np.arange(cell_count * RATIO)
    parent = fine_cell // RATIO
    offset = (fine_cell % RATIO + 0.5) / RATIO - 0.5
    table = np.zeros((LANES, cell_count * RATIO), np.float32)
    table[parent + 1, fine_cell] = 1.0 - np.abs(offset)
    table[np.where(offset > 0, parent + 2, parent), fine_cell] = np.abs(offset)
    return np.concatenate([table, table], axis=0).astype(jnp.bfloat16)


def average_table(fine_count, weight):
    cell = np.arange(fine_count // RATIO)[None, :]
    table = np.where(np.arange(fine_count)[:, None] // RATIO == cell, weight, 0.0)
    return np.concatenate([table, table], axis=0).astype(jnp.bfloat16)


def split_parts(value):
    high = value.astype(jnp.bfloat16)
    return high, (value - high.astype(jnp.float32)).astype(jnp.bfloat16)


def product(left, right):
    return jnp.dot(left, right, preferred_element_type=jnp.float32)


def split_pair(value, axis):
    return jnp.concatenate(split_parts(value), axis=axis)


def block_means(total, rows_ref, lanes_ref):
    half = product(rows_ref[...], split_pair(total, 0))
    fine = LANES * RATIO
    chunks = half.shape[1] // fine
    stacked = jnp.concatenate([half[:, k * fine : (k + 1) * fine] for k in range(chunks)], axis=0)
    cells = product(split_pair(stacked, 1), lanes_ref[...])
    height = half.shape[0]
    return [cells[k * height : (k + 1) * height] for k in range(chunks)]


def fine_kernel(
    rate_ref,
    cells_hbm,
    edge_ref,
    south_ref,
    north_ref,
    under_hbm,
    over_hbm,
    rim_ref,
    heat_ref,
    ty_ref,
    tx_ref,
    ry_ref,
    rx_ref,
    out_hbm,
    coarse_ref,
    factor_ref,
    held,
    vel,
    acc,
    ready,
    in_sem,
    out_sem,
):
    plane = pl.program_id(0)
    slabs, spans, tall = held.shape[:3]
    levels, rows, cols = cells_hbm.shape
    strips, tiles = rows // SUBLANES, cols // LANES
    fields = rim_ref.shape[0]
    pieces = vel.shape[0]
    half = LANES // 2

    early = over_hbm.shape[1]

    near = min(RATIO + 1, levels)
    groups = (
        (under_hbm, 0, 1, 0),
        (cells_hbm, 0, near, 1),
        (cells_hbm, near, levels - near, near + 1),
        (over_hbm, 0, 1, slabs - 1),
    )

    def start_group(k):
        source, first, depth, slab = groups[k]

        @pl.loop(0, tiles if depth else 0)
        def _(tile):
            pltpu.make_async_copy(
                source.at[
                    pl.ds(first, depth), :, pl.ds(pl.multiple_of(tile * LANES, LANES), LANES)
                ],
                held.at[pl.ds(slab, depth), tile, pl.ds(SUBLANES, source.shape[1]), :],
                in_sem.at[k],
            ).start()

    def wait_group(k):
        source, _, depth, slab = groups[k]
        if depth:
            whole = held.at[
                pl.ds(slab, depth), pl.ds(0, tiles), pl.ds(SUBLANES, source.shape[1]), :
            ]
            pltpu.make_async_copy(whole, whole, in_sem.at[k]).wait()

    @pl.when(plane == 0)
    def _():
        start_group(0)
        start_group(1)
        empty = jnp.zeros((tiles, rows - early, LANES), jnp.float32)
        held[slabs - 1, 0:tiles, SUBLANES + early : SUBLANES + rows, :] = empty

    for part in range(RATIO):
        level = plane * RATIO + part
        held[level + 1, tiles, SUBLANES : SUBLANES + rows, :] = edge_ref[part]
        for tile in range(tiles):
            lanes = slice(tile * LANES, (tile + 1) * LANES)
            held[level + 1, tile, SUBLANES - 1 : SUBLANES, :] = south_ref[part, :, lanes]
            held[level + 1, tile, SUBLANES + rows : SUBLANES + rows + 1, :] = north_ref[part, :, lanes]

    along = jnp.concatenate(
        [product(ty_ref[...], split_pair(rim_ref[field, 0], 0)) for field in range(fields)],
        axis=0,
    )
    span = along.shape[1]
    views = [split_parts(along), split_parts(pltpu.roll(along, span - half, 1))]
    group = min(4, pieces)
    for first in range(0, pieces, group):
        windows = []
        for k in range(first, first + group):
            high, low = views[k % 2]
            lanes = slice(k // 2 * LANES, (k // 2 + 1) * LANES)
            windows.append(jnp.concatenate([high[:, lanes], low[:, lanes]], axis=1))
        refined = product(jnp.concatenate(windows, axis=0), tx_ref[...])
        for k in range(group):
            vel[first + k] = refined[k * fields * rows : (k + 1) * fields * rows]

    @pl.when(plane == 0)
    def _():
        start_group(2)
        start_group(3)
        wait_group(0)
        wait_group(1)

    top_plane = plane == pl.num_programs(0) - 1

    @pl.when(plane == (1 if levels > RATIO else 0))
    def _():
        wait_group(2)
        wait_group(3)

    side_rates = [fine_step * rate_ref[plane * RATIO + part] for part in range(RATIO)]
    own_rates = [1.0 - 6.0 * rate for rate in side_rates]
    lane_at = lax.broadcasted_iota(jnp.int32, (SUBLANES, LANES), 1)
    first_lane, last_lane = lane_at == 0, lane_at == LANES - 1
    per_turn = vel.shape[2] // LANES
    base = plane * RATIO

    def out_copy(index, strip):
        at = pl.ds(pl.multiple_of(strip * SUBLANES, SUBLANES), SUBLANES)
        block = pl.ds(index * RATIO, RATIO)
        return pltpu.make_async_copy(
            ready.at[block, at, :], out_hbm.at[block, at, :], out_sem.at[index, strip]
        )

    @pl.loop(0, strips)
    def _(s):
        start = pl.multiple_of(s * SUBLANES, SUBLANES)
        at = pl.ds(start, SUBLANES)
        middle = pl.ds(start + SUBLANES, SUBLANES)
        below, above = pl.ds(start + SUBLANES - 1, SUBLANES), pl.ds(start + SUBLANES + 1, SUBLANES)
        slabs_here = [base + part + 1 for part in range(RATIO)]
        west_turned = [pltpu.roll(held[slab, tiles, middle, :], 1, 1) for slab in slabs_here]
        centre = [held[slab, 0, middle, :] for slab in slabs_here]
        east_turned = [pltpu.roll(x, LANES - 1, 1) for x in centre]
        for tile in range(tiles):
            k, j = divmod(tile, per_turn)
            lanes = slice(tile * LANES, (tile + 1) * LANES)
            inner = slice(j * LANES, (j + 1) * LANES)
            ahead = [held[slab, tile + 1, middle, :] for slab in slabs_here]
            ahead_turned = [pltpu.roll(x, LANES - 1, 1) for x in ahead]
            here_turned = [pltpu.roll(x, 1, 1) for x in centre]
            column = (
                [held[base, tile, middle, :]] + centre + [held[base + RATIO + 1, tile, middle, :]]
            )
            flow = [
                vel[k, pl.ds(pl.multiple_of(f * rows + start, SUBLANES), SUBLANES), inner]
                for f in range(fields)
            ]
            total = None
            for part, slab in enumerate(slabs_here):
                west = jnp.where(first_lane, west_turned[part], here_turned[part])
                east = jnp.where(last_lane, ahead_turned[part], east_turned[part])
                south, north = held[slab, tile, below, :], held[slab, tile, above, :]
                lower, upper = column[part], column[part + 2]
                around = (east + west) + (north + south) + (upper + lower)
                advection = (
                    flow[0] * (east - west)
                    + flow[1] * (north - south)
                    + flow[2] * (upper - lower)
                )
                updated = own_rates[part] * centre[part] + side_rates[part] * around - advection
                ready[base + part, at, lanes] = updated
                total = updated if total is None else total + updated
            acc[at, lanes] = total
            west_turned, centre, east_turned = here_turned, ahead, ahead_turned
        out_copy(plane, s).start()

    for k, cells in enumerate(block_means(acc[...], ry_ref, rx_ref)):
        lanes = slice(k * LANES, (k + 1) * LANES)
        coarse_ref[0, :, lanes] = heat_ref[0, :, lanes] - cells

    @pl.when(top_plane)
    def _():
        wide = vel.shape[2]
        for k in range(pieces):
            factor_ref[:, k * wide : (k + 1) * wide] = (
                side_rates[RATIO - 1] - vel[k, (fields - 1) * rows + early : fields * rows, :]
            )

    @pl.when(top_plane)
    def _():
        for index in range(levels // RATIO):
            for s in range(strips):
                out_copy(index, s).wait()


def fine_update(rimmed, heat, edge, south, north, under, over, salinity, diffusivity):
    levels, rows, cols = salinity.shape
    fields, quarter = rimmed.shape[:2]
    row_count, width = rows // RATIO, cols // RATIO
    cell_count = LANES // 2
    late_rows = rows - over.shape[1]
    ty = rows_table(row_count, rimmed.shape[2])
    tx = lanes_table(cell_count)
    ry = average_table(rows, 1.0 / RATIO).T
    rx = average_table(LANES * RATIO, 1.0 / RATIO / RATIO)
    pieces = width // cell_count

    def fixed(array):
        return pl.BlockSpec(array.shape, lambda i: (0,) * array.ndim)

    hbm = pl.BlockSpec(memory_space=pltpu.HBM)
    return pl.pallas_call(
        fine_kernel,
        name="fine_levels",
        grid=(quarter,),
        in_specs=[
            pl.BlockSpec(memory_space=pltpu.SMEM),
            hbm,
            pl.BlockSpec((RATIO, rows, LANES), lambda i: (i, 0, 0)),
            pl.BlockSpec((RATIO, 1, cols), lambda i: (i, 0, 0)),
            pl.BlockSpec((RATIO, 1, cols), lambda i: (i, 0, 0)),
            hbm,
            hbm,
            pl.BlockSpec((fields, 1) + rimmed.shape[2:], lambda i: (0, i, 0, 0)),
            pl.BlockSpec((1, row_count, width), lambda i: (i, 0, 0)),
            fixed(ty),
            fixed(tx),
            fixed(ry),
            fixed(rx),
        ],
        out_specs=[
            hbm,
            pl.BlockSpec((1, row_count, width), lambda i: (i, 0, 0)),
            pl.BlockSpec((late_rows, cols), lambda i: (0, 0)),
        ],
        out_shape=[
            jax.ShapeDtypeStruct(salinity.shape, jnp.float32),
            jax.ShapeDtypeStruct((quarter, row_count, width), jnp.float32),
            jax.ShapeDtypeStruct((late_rows, cols), jnp.float32),
        ],
        scratch_shapes=[
            pltpu.VMEM((levels + 2, cols // LANES + 1, rows + 2 * SUBLANES, LANES), jnp.float32),
            pltpu.VMEM((pieces, fields * rows, cell_count * RATIO), jnp.float32),
            pltpu.VMEM((rows, cols), jnp.float32),
            pltpu.VMEM((levels, rows, cols), jnp.float32),
            pltpu.SemaphoreType.DMA((4,)),
            pltpu.SemaphoreType.DMA((quarter, rows // SUBLANES)),
        ],
        compiler_params=pltpu.CompilerParams(
            dimension_semantics=("arbitrary",), vmem_limit_bytes=59 * 2**20
        ),
        cost_estimate=pl.CostEstimate(flops=10**9, bytes_accessed=4 * 10**7, transcendentals=0),
    )(diffusivity, salinity, edge, south, north, under, over, rimmed, heat, ty, tx, ry, rx)


def outer_kernel(
    level_hbm,
    factor_hbm,
    over_hbm,
    cells_hbm,
    ry_hbm,
    rx_hbm,
    out_hbm,
    coarse_ref,
    held,
    factor_ref,
    over_ref,
    ry_ref,
    rx_ref,
    in_sem,
    out_sem,
):
    levels, rows = out_hbm.shape[:2]
    late = held.shape[0]
    plane = coarse_ref.shape[0] - 1
    place = out_hbm.at[levels - 1, pl.ds(rows - late, late), :]
    pairs = (
        (factor_hbm, factor_ref),
        (over_hbm.at[0], over_ref),
        (ry_hbm, ry_ref),
        (rx_hbm, rx_ref),
        (place, held),
        (cells_hbm, coarse_ref),
    )
    loads = [
        pltpu.make_async_copy(source, target, in_sem.at[k])
        for k, (source, target) in enumerate(pairs)
    ]
    for load in loads:
        load.start()
    for load in loads:
        load.wait()
    added = factor_ref[...] * over_ref[...]
    held[...] = held[...] + added
    store = pltpu.make_async_copy(held, place, out_sem.at[0])
    store.start()
    for k, cells in enumerate(block_means(added, ry_ref, rx_ref)):
        lanes = slice(k * LANES, (k + 1) * LANES)
        coarse_ref[plane, :, lanes] = coarse_ref[plane, :, lanes] - cells
    store.wait()


def outer_update(levels_next, factor, over, cells):
    rows = levels_next.shape[1]
    late = factor.shape[0]
    ry = average_table(rows, 1.0 / RATIO)[rows - late : rows].T
    ry = np.concatenate([ry, ry], axis=1)
    rx = average_table(LANES * RATIO, 1.0 / RATIO / RATIO)
    hbm = pl.BlockSpec(memory_space=pltpu.HBM)
    return pl.pallas_call(
        outer_kernel,
        name="outer_levels",
        in_specs=[hbm] * 6,
        out_specs=[hbm, pl.BlockSpec(memory_space=pltpu.VMEM)],
        out_shape=[
            jax.ShapeDtypeStruct(levels_next.shape, jnp.float32),
            jax.ShapeDtypeStruct(cells.shape, jnp.float32),
        ],
        scratch_shapes=[
            pltpu.VMEM(factor.shape, jnp.float32),
            pltpu.VMEM(factor.shape, jnp.float32),
            pltpu.VMEM(factor.shape, jnp.float32),
            pltpu.VMEM(ry.shape, jnp.bfloat16),
            pltpu.VMEM(rx.shape, jnp.bfloat16),
            pltpu.SemaphoreType.DMA((6,)),
            pltpu.SemaphoreType.DMA((1,)),
        ],
        input_output_aliases={0: 0},
        compiler_params=pltpu.CompilerParams(vmem_limit_bytes=24 * 2**20),
        cost_estimate=pl.CostEstimate(flops=10**8, bytes_accessed=4 * 10**6, transcendentals=0),
    )(levels_next, factor, over, cells, ry, rx)


def from_above(layer, axis):
    count = lax.axis_size(axis)
    return lax.ppermute(layer, axis, [((i + 1) % count, i) for i in range(count)])


def per_device(coarse_modes, salinity, viscosity, forcing_gain, diffusivity):
    width = coarse_modes.shape[4]
    groups, columns = lax.axis_size("grp"), lax.axis_size("gx")
    early_rows = salinity.shape[1] - LATE_PIECES * SUBLANES
    rimmed, heat, edge, south, north, under, over, low = forward(
        coarse_modes[0], salinity, early_rows, groups, columns, lax.axis_size("gy")
    )
    over_late = from_above(low, "grp")
    partial_next, partial_cells, factor = fine_update(
        rimmed, heat, edge, south, north, under, over, salinity, diffusivity
    )
    salinity_next, restricted = outer_update(partial_next, factor, over_late, partial_cells)
    total_modes = width * columns
    mode_index = lax.axis_index("gx") * width + lax.broadcasted_iota(jnp.int32, (1, width), 1)
    wavenumber = jnp.where(mode_index < total_modes // 2, mode_index, mode_index - total_modes)
    scaled_wave = 2.0 * math.pi / total_modes * wavenumber.astype(jnp.float32)
    damping = jnp.exp(-viscosity[0] * scaled_wave * scaled_wave)
    coarse_next = backward(forcing_gain, restricted, coarse_modes[0], damping, groups, columns)
    return (salinity_next, coarse_next[None])


def solution(mesh):
    return jax.shard_map(
        per_device,
        mesh=mesh,
        in_specs=(
            P("grp", None, None, "gy", "gx"),
            P("grp", "gy", "gx"),
            P("grp"),
            P("grp"),
            P("grp"),
        ),
        out_specs=(P("grp", "gy", "gx"), P("grp", None, None, "gy", "gx")),
        check_vma=False,
    )
```
